256 devices in a mesh: leaf: 64 (over x, z, core), col: 4 (over y).
Axes of the slice: x: 4, y: 4, z: 8, core: 2. Of those that a mesh axis runs over, the one named last changes fastest.
Arguments:
- right_side: bfloat16 [131072, 256], P('leaf'), may hold values from -6 to 6
- x_blocks: bfloat16 [64, 4, 96, 128, 128], P('leaf', 'col'), may hold values from -0.109375 to 0.109375
- row_ids: int32 [64, 4, 96], P('leaf', 'col'), may hold values from 0 to 15
- col_ids: int32 [64, 4, 96], P('leaf', 'col'), may hold values from 0 to 13
- counts: int32 [64, 4], P('leaf', 'col'), may hold values from 48 to 96, as said below
Outputs:
- solution: bfloat16 [131072, 256], P(('leaf', 'col'))
The draws below stay inside these ranges and needn't reach their ends.
Inputs may be any that keep to these rules, and one draw needn't show every extreme that they name: `row_ids`: block rows index the rows of the device's own subtree. `col_ids`: slots below 2 are the subtree's own columns; slot 2 + (l - 1) * 2 + s is column s of the level-l separator. `counts`: some device uses all 96 slots; slots past a device's count are unused.
All inputs are finite; a program needn't handle non-finite values.
Results may differ from the reference program's by a relative error of at most 0.0047.
Values may be sent and summed in bfloat16 or wider, within the bound.
A program may use at most 128 MiB of HBM per device.

```python
import jax
import jax.numpy as jnp
from jax import lax

BLOCK = 128
K = 256
RB_DEV = 16
NBLK = 96
CI = 2
SEP = 2
LEVELS = 6
CT = 14
ORDER = 131072
N_LEAF = 64
N_COL = 4


def draw_counts(key, part):
    first_key = jax.random.fold_in(key, 11)
    second_key = jax.random.fold_in(key, 12)
    third_key = jax.random.fold_in(key, 13)
    values = jax.random.randint(first_key, (N_LEAF * N_COL,), NBLK // 2, NBLK + 1)
    fullest = jax.random.randint(second_key, (), 0, N_LEAF * N_COL)
    emptiest = (fullest + 1 + jax.random.randint(third_key, (), 0, N_LEAF * N_COL - 1)) % (N_LEAF * N_COL)
    positions = jnp.arange(N_LEAF * N_COL)
    values = jnp.where(positions == fullest, NBLK, values)
    values = jnp.where(positions == emptiest, NBLK // 2, values)
    return values.reshape(N_LEAF, N_COL).astype(jnp.int32)


def plant(array, own_key, least, top_value):
    longest = array.shape.index(max(array.shape))
    spots = []
    for shift in (0, 1):
        where = [jax.random.randint(jax.random.fold_in(own_key, axis), (), 0, length) for axis, length in enumerate(array.shape)]
        where[longest] = (where[longest] + shift) % array.shape[longest]
        spots.append(tuple(where))
    return array.at[spots[0]].set(least).at[spots[1]].set(top_value)


def shard_levels(rng, dims, cuts, smallest, largest):
    factor_of, own = 1.0, jax.random.fold_in(rng, 6)
    for axis_at, parts in cuts:
        draws = jnp.exp(jax.random.uniform(jax.random.fold_in(own, axis_at), (parts,), jnp.float32, smallest / len(cuts), largest / len(cuts)))
        factor_of = factor_of * jnp.repeat(draws, dims[axis_at] // parts).reshape([-1 if axis == axis_at else 1 for axis in range(len(dims))])
    return factor_of


def bell_draw(rng, extent, width, most, shards=(), kind=jnp.bfloat16):
    array = jax.random.normal(rng, extent, jnp.float32) * width
    if len(shards) > 0:
        array = shard_levels(rng, extent, shards, -0.22, 0.18) * array
    return jnp.clip(array, min=-most, max=most).astype(kind)


def setup_inputs(seed: int = 0) -> dict:
    splits = jax.random.split(jax.random.key(seed), 6)
    return {
        "right_side": bell_draw(splits[0], (ORDER, K), 1.0, 6.0, ((0, 64),)),
        "x_blocks": bell_draw(splits[1], (N_LEAF, N_COL, NBLK, BLOCK, BLOCK), (BLOCK * NBLK // 4) ** -0.5, 0.109375, ((0, 64), (1, 4))),
        "row_ids": plant(jax.random.randint(splits[2], (N_LEAF, N_COL, NBLK), 0, RB_DEV), jax.random.fold_in(splits[2], 1), 0, RB_DEV - 1).astype(jnp.int32),
        "col_ids": plant(jax.random.randint(splits[3], (N_LEAF, N_COL, NBLK), 0, CT), jax.random.fold_in(splits[3], 1), 0, CT - 1).astype(jnp.int32),
        "counts": draw_counts(jax.random.fold_in(splits[5], 71), 0),
    }


def reference(right_side, x_blocks, row_ids, col_ids, counts):
    num_leaf, num_col, list_len, block_size, _ = x_blocks.shape
    columns = right_side.shape[1]
    rhs_blocks = right_side.reshape(num_leaf, RB_DEV, block_size, columns)
    slot_ids = jnp.arange(list_len, dtype=jnp.int32)
    alive_mask = slot_ids[None, None, :] < counts[:, :, None]
    flat_blocks = x_blocks.reshape(num_leaf * num_col, list_len, block_size, block_size)
    flat_rows = row_ids.reshape(num_leaf * num_col, list_len)
    flat_cols = col_ids.reshape(num_leaf * num_col, list_len)
    flat_alive = alive_mask.reshape(num_leaf * num_col, list_len)
    device_ids = jnp.arange(num_leaf * num_col, dtype=jnp.int32)
    high = lax.Precision.HIGHEST

    def local_partial(items):
        blocks, block_rows, block_cols, alive, device = items
        mine = rhs_blocks[device // num_col]
        picked = mine[block_rows].astype(jnp.float32)
        products = jnp.einsum("kab,kac->kbc", blocks.astype(jnp.float32), picked, precision=high)
        col_select = ((block_cols[None, :] == jnp.arange(CT, dtype=jnp.int32)[:, None]) & alive[None, :]).astype(jnp.float32)
        return jnp.einsum("ck,kbd->cbd", col_select, products, precision=high)

    partial_value = lax.map(local_partial, (flat_blocks, flat_rows, flat_cols, flat_alive, device_ids))
    partial_value = partial_value.reshape(num_leaf, num_col, CT, block_size, columns)
    pieces = [partial_value[:, :, :CI]]
    for level in range(1, LEVELS + 1):
        group = 2 ** level
        segment = partial_value[:, :, CI + (level - 1) * SEP: CI + level * SEP]
        segment = segment.reshape(num_leaf // group, group, num_col, SEP, block_size, columns)
        summed = jnp.sum(segment, axis=1, keepdims=True)
        summed = jnp.broadcast_to(summed, segment.shape).reshape(num_leaf, num_col, SEP, block_size, columns)
        pieces.append(summed)
    combined = jnp.concatenate(pieces, axis=2)
    coarse = combined.astype(jnp.bfloat16).reshape(num_leaf * num_col, CT, block_size, columns)

    def local_terms(items):
        blocks, block_rows, block_cols, alive, coarse_dev = items
        gathered = coarse_dev[block_cols].astype(jnp.float32)
        image = jnp.einsum("kab,kbc->kac", blocks.astype(jnp.float32), gathered, precision=high)
        row_select = ((block_rows[None, :] == jnp.arange(RB_DEV, dtype=jnp.int32)[:, None]) & alive[None, :]).astype(jnp.float32)
        return jnp.einsum("rk,kac->rac", row_select, image, precision=high)

    terms = lax.map(local_terms, (flat_blocks, flat_rows, flat_cols, flat_alive, coarse))
    terms = terms.reshape(num_leaf, num_col, RB_DEV, block_size, columns)
    total = jnp.sum(terms, axis=1)
    return total.reshape(num_leaf * RB_DEV * block_size, columns).astype(jnp.bfloat16)
```

```python
import jax
import jax.numpy as jnp
from jax import lax
from jax.experimental import pallas as pl
from jax.experimental.pallas import tpu as pltpu
from jax.sharding import PartitionSpec as P

BLOCK = 128
ROW_BLOCKS = 16
LIST_LEN = 96
COLUMNS = 256
SLOTS = 14
ROWS = ROW_BLOCKS * BLOCK
WIDTH = SLOTS * BLOCK
Z = 8
X = 4
HALF = COLUMNS // 2
MESH = pl.DeviceIdType.MESH
GROUPS = 8
PER_GROUP = LIST_LEN // GROUPS
F32 = jnp.float32
BF16 = jnp.bfloat16


def build_kernel(row_ref, col_ref, count_ref, right_hbm, blocks_hbm, dense, right_t, right_buf, block_buf, extra, seen, sems):
    fetch_right = pltpu.make_async_copy(right_hbm, right_buf, sems.at[GROUPS])
    fetch_right.start()
    fetches = []
    for g in range(GROUPS):
        part = pl.ds(g * PER_GROUP, PER_GROUP)
        fetches.append(pltpu.make_async_copy(blocks_hbm.at[0, 0, part], block_buf.at[part], sems.at[g]))
        fetches[-1].start()

    @pl.loop(0, ROW_BLOCKS * SLOTS)
    def _(p):
        seen[p] = -1

    @pl.loop(0, ROWS // 64)
    def _(i):
        dense[pl.ds(pl.multiple_of(i * 64, 64), 64), :] = jnp.zeros((64, WIDTH), BF16)

    fetch_right.wait()

    @pl.loop(0, ROW_BLOCKS)
    def _(i):
        at = pl.multiple_of(i * BLOCK, BLOCK)
        right_t[:, pl.ds(at, BLOCK)] = right_buf[pl.ds(at, BLOCK), :].T

    count = count_ref[0, 0]
    used = jnp.int32(0)
    for g in range(GROUPS):
        fetches[g].wait()

        def add_block(k, used):
            r = row_ref[0, 0, k]
            c = col_ref[0, 0, k]
            place = r * SLOTS + c
            state = seen[place]
            rows = pl.ds(pl.multiple_of(r * BLOCK, BLOCK), BLOCK)
            cols = pl.ds(pl.multiple_of(c * BLOCK, BLOCK), BLOCK)

            @pl.when(state == -1)
            def _():
                dense[rows, cols] = block_buf[k]
                seen[place] = -2

            @pl.when(state == -2)
            def _():
                total = dense[rows, cols].astype(F32) + block_buf[k].astype(F32)
                extra[used] = total
                dense[rows, cols] = total.astype(BF16)
                seen[place] = used

            @pl.when(state >= 0)
            def _():
                total = extra[state] + block_buf[k].astype(F32)
                extra[state] = total
                dense[rows, cols] = total.astype(BF16)

            return used + jnp.where(state == -2, 1, 0)

        used = lax.fori_loop(g * PER_GROUP, jnp.clip(count, g * PER_GROUP, (g + 1) * PER_GROUP), add_block, used)


def level_lanes(level, levels=1):
    start = (2 + (level - 1) * 2) * BLOCK
    return slice(start, start + levels * 2 * BLOCK)


TOP = level_lanes(5, 2)
LOW = TOP.start


def dot_t(a, b):
    return lax.dot_general(a, b, (((1,), (1,)), ((), ())), preferred_element_type=F32)


def solve_kernel(
    dense, right_t, out,
    coarse, pair_out, pair_in, own, z_out, z_in, quad_in, next_in, x_out, x_in,
    terms, y_far, y_far_in, y_out, y_in, send, recv,
):
    leaf = lax.axis_index("leaf")
    col = lax.axis_index("col")
    core = lax.rem(leaf, 2)
    z = lax.rem(leaf // 2, Z)
    x = leaf // (2 * Z)
    quad = z // 4
    in_quad = lax.rem(z, 4)

    def at(x_to, z_to, core_to):
        return ((x_to * Z + z_to) * 2 + core_to, col)

    partner = at(x, z, 1 - core)
    z_peer = [at(x, lax.rem(z + d, Z), core) for d in range(Z)]
    quad_peer = [at(x, quad * 4 + lax.rem(in_quad + d, 4), core) for d in range(4)]
    z_next = z + 1 - 2 * lax.rem(z, 2)
    x_peer = []
    for b in range(X):
        flip_0 = x + 1 - 2 * lax.rem(x, 2) if b & 1 else x
        high = flip_0 // 2
        flip_1 = flip_0 + 2 - 4 * high if b & 2 else flip_0
        x_peer.append(at(flip_1, z, core))
    up = (leaf, lax.rem(col + 1, 4))
    down = (leaf, lax.rem(col + 3, 4))

    barrier = pltpu.get_barrier_semaphore()
    peers = [partner] + z_peer[1:] + x_peer[1:] + [up, down]
    for peer in peers:
        pl.semaphore_signal(barrier, inc=1, device_id=peer, device_id_type=MESH)

    started = []

    def copy(src, dst, to):
        n = len(started)
        c = pltpu.make_async_remote_copy(
            src_ref=src, dst_ref=dst, send_sem=send.at[n], recv_sem=recv.at[n], device_id=to, device_id_type=MESH
        )
        c.start()
        started.append(c)
        return c

    mine = pl.ds(pl.multiple_of(core * HALF, HALF), HALF)
    other = pl.ds(pl.multiple_of((1 - core) * HALF, HALF), HALF)

    def pair_start(lanes):
        value = lax.dot_general(right_t[...], dense[:, lanes], (((1,), (0,)), ((), ())), preferred_element_type=F32)
        own[:, lanes] = value
        pair_out[:, lanes] = value.astype(BF16)

    def pair_send(lanes):
        return copy(pair_out.at[other, lanes], pair_in.at[:, lanes], partner)

    def pair_sum(lanes):
        return own[mine, lanes] + pair_in[:, lanes].astype(F32)

    pair_start(TOP)
    pl.semaphore_wait(barrier, len(peers))
    pair_top = pair_send(TOP)
    low_pairs = {}
    for level in (4, 3, 2):
        pair_start(level_lanes(level))
        low_pairs[level] = pair_send(level_lanes(level))

    def keep(lanes, total):
        own[mine, lanes] = total
        z_out[:, lanes] = total.astype(BF16)

    def ring_send(lanes):
        copies = []
        for d in range(1, Z):
            rows = pl.ds(pl.multiple_of(lax.rem(z + d, Z) * 16, 16), 16)
            copies.append(copy(z_out.at[rows, lanes], z_in.at[d, :, lanes], z_peer[d]))
        return copies

    chunk = pl.ds(pl.multiple_of(core * HALF + z * 16, 16), 16)

    def ring_sum(copies, lanes):
        total = own[chunk, lanes]
        for d in range(1, Z):
            copies[d - 1].wait_recv()
            total += z_in[d, :, lanes].astype(F32)
        return total

    def ring_share(lanes):
        return [copy(coarse.at[chunk, lanes], coarse.at[chunk, lanes], z_peer[d]) for d in range(1, Z)]

    pair_top.wait_recv()
    keep(TOP, pair_sum(TOP))
    top_ring = ring_send(TOP)

    four = level_lanes(4)
    low_pairs[4].wait_recv()
    keep(four, pair_sum(four))
    four_ring = ring_send(four)

    three = level_lanes(3)
    low_pairs[3].wait_recv()
    keep(three, pair_sum(three))
    three_quad = []
    for d in range(1, 4):
        rows = pl.ds(pl.multiple_of(lax.rem(in_quad + d, 4) * 32, 32), 32)
        three_quad.append(copy(z_out.at[rows, three], quad_in.at[d], quad_peer[d]))

    two = level_lanes(2)
    low_pairs[2].wait_recv()
    keep(two, pair_sum(two))
    two_next = copy(z_out.at[:, two], next_in, at(x, z_next, core))

    one = level_lanes(1)
    pair_start(slice(0, one.stop))
    one_pair = copy(pair_out.at[:, one], y_far_in.at[2], partner)
    coarse[:, 0:one.start] = pair_out[:, 0:one.start]

    top_chunk = ring_sum(top_ring, TOP)
    x_out[...] = top_chunk
    six = slice(2 * BLOCK, 4 * BLOCK)
    x_copies = [
        copy(x_out, x_in.at[1], x_peer[1]),
        copy(x_out.at[:, six], x_in.at[2, :, six], x_peer[2]),
        copy(x_out.at[:, six], x_in.at[3, :, six], x_peer[3]),
    ]

    coarse[chunk, four] = ring_sum(four_ring, four).astype(BF16)
    four_share = ring_share(four)

    quad_rows = pl.ds(pl.multiple_of(core * HALF + in_quad * 32, 32), 32)
    total = own[quad_rows, three]
    for d in range(1, 4):
        three_quad[d - 1].wait_recv()
        total += quad_in[d].astype(F32)
    coarse[quad_rows, three] = total.astype(BF16)
    three_share = [copy(coarse.at[quad_rows, three], coarse.at[quad_rows, three], quad_peer[d]) for d in range(1, 4)]

    for c in x_copies:
        c.wait_recv()
    coarse[chunk, TOP.start:TOP.start + 2 * BLOCK] = (x_out[:, 0:2 * BLOCK] + x_in[1, :, 0:2 * BLOCK]).astype(BF16)
    coarse[chunk, TOP.start + 2 * BLOCK:TOP.stop] = (
        (x_out[:, six] + x_in[1, :, six]) + (x_in[2, :, six] + x_in[3, :, six])
    ).astype(BF16)
    top_share = ring_share(TOP)

    two_next.wait_recv()
    coarse[mine, two] = (own[mine, two] + next_in[...].astype(F32)).astype(BF16)
    give_two = copy(coarse.at[mine, two], coarse.at[mine, two], partner)
    one_pair.wait_recv()
    coarse[:, one] = (own[:, one] + y_far_in[2].astype(F32)).astype(BF16)
    for c in three_share:
        c.wait_recv()
    give_three = copy(coarse.at[mine, three], coarse.at[mine, three], partner)
    for c in four_share:
        c.wait_recv()
    give_four = copy(coarse.at[mine, four], coarse.at[mine, four], partner)
    for c in (give_two, give_three, give_four):
        c.wait_recv()

    @pl.loop(0, ROWS // 256)
    def _(i):
        rows = pl.ds(pl.multiple_of(i * 256, 256), 256)
        terms[rows, :] = dot_t(dense[rows, 0:LOW], coarse[:, 0:LOW])

    for c in top_share:
        c.wait_recv()
    give_top = copy(coarse.at[mine, TOP], coarse.at[mine, TOP], partner)
    give_top.wait_recv()

    def finish(quarter, half):
        rows = pl.ds(pl.multiple_of(quarter * 512 + half * 256, 256), 256)
        return terms[rows, :] + dot_t(dense[rows, TOP], coarse[:, TOP])

    far = lax.rem(col + 2, 4)
    above = lax.rem(col + 1, 4)
    below = lax.rem(col + 3, 4)
    y_far[0] = finish(far, 0).astype(BF16)
    far_up = copy(y_far.at[0], y_far_in.at[0], up)
    y_far[1] = finish(far, 1).astype(BF16)
    far_down = copy(y_far.at[1], y_far_in.at[1], down)
    y_out[0, 1] = finish(above, 1).astype(BF16)
    up_b = copy(y_out.at[0, 1], y_in.at[0, 1], up)
    y_out[1, 0] = finish(below, 0).astype(BF16)
    down_a = copy(y_out.at[1, 0], y_in.at[1, 0], down)
    up_value = finish(above, 0)
    far_up.wait_recv()
    y_out[0, 0] = (up_value + y_far_in[0].astype(F32)).astype(BF16)
    up_a = copy(y_out.at[0, 0], y_in.at[0, 0], up)
    down_value = finish(below, 1)
    far_down.wait_recv()
    y_out[1, 1] = (down_value + y_far_in[1].astype(F32)).astype(BF16)
    down_b = copy(y_out.at[1, 1], y_in.at[1, 1], down)
    for half in range(2):
        rows = pl.ds(pl.multiple_of(col * 512 + half * 256, 256), 256)
        terms[rows, :] = finish(col, half)
    for half, pair in ((1, (up_b, down_b)), (0, (up_a, down_a))):
        for c in pair:
            c.wait_recv()
        rows = pl.ds(pl.multiple_of(col * 512 + half * 256, 256), 256)
        total = terms[rows, :] + (y_in[0, half].astype(F32) + y_in[1, half].astype(F32))
        out[half * 256:(half + 1) * 256, :] = total.astype(BF16)
    for c in started:
        c.wait_send()


COPIES = 80


def body(right_side, x_blocks, row_ids, col_ids, counts):
    vmem = pl.BlockSpec(memory_space=pltpu.VMEM)
    smem = pl.BlockSpec(memory_space=pltpu.SMEM)
    hbm = pl.BlockSpec(memory_space=pl.ANY)
    dense, right_t = pl.pallas_call(
        build_kernel,
        out_shape=(jax.ShapeDtypeStruct((ROWS, WIDTH), BF16), jax.ShapeDtypeStruct((COLUMNS, ROWS), BF16)),
        in_specs=[smem, smem, smem, hbm, hbm],
        out_specs=(vmem, vmem),
        scratch_shapes=[
            pltpu.VMEM((ROWS, COLUMNS), BF16),
            pltpu.VMEM((LIST_LEN, BLOCK, BLOCK), BF16),
            pltpu.VMEM((LIST_LEN // 2, BLOCK, BLOCK), F32),
            pltpu.SMEM((ROW_BLOCKS * SLOTS,), jnp.int32),
            pltpu.SemaphoreType.DMA((GROUPS + 1,)),
        ],
        compiler_params=pltpu.CompilerParams(vmem_limit_bytes=20 * 2**20),
        name="build_dense",
    )(row_ids, col_ids, counts, right_side, x_blocks)
    return pl.pallas_call(
        solve_kernel,
        out_shape=jax.ShapeDtypeStruct((ROWS // 4, COLUMNS), BF16),
        in_specs=[vmem, vmem],
        out_specs=vmem,
        scratch_shapes=[
            pltpu.VMEM((COLUMNS, WIDTH), BF16),
            pltpu.VMEM((COLUMNS, WIDTH), BF16),
            pltpu.VMEM((HALF, WIDTH), BF16),
            pltpu.VMEM((COLUMNS, WIDTH), F32),
            pltpu.VMEM((HALF, WIDTH), BF16),
            pltpu.VMEM((Z, 16, WIDTH), BF16),
            pltpu.VMEM((4, 32, 2 * BLOCK), BF16),
            pltpu.VMEM((HALF, 2 * BLOCK), BF16),
            pltpu.VMEM((16, 4 * BLOCK), F32),
            pltpu.VMEM((X, 16, 4 * BLOCK), F32),
            pltpu.VMEM((ROWS, COLUMNS), F32),
            pltpu.VMEM((2, 256, COLUMNS), BF16),
            pltpu.VMEM((3, 256, COLUMNS), BF16),
            pltpu.VMEM((2, 2, 256, COLUMNS), BF16),
            pltpu.VMEM((2, 2, 256, COLUMNS), BF16),
            pltpu.SemaphoreType.DMA((COPIES,)),
            pltpu.SemaphoreType.DMA((COPIES,)),
        ],
        compiler_params=pltpu.CompilerParams(
            collective_id=0, has_side_effects=True, vmem_limit_bytes=32 * 2**20
        ),
        name="solve",
    )(dense, right_t)


def solution(mesh):
    in_specs = (
        P("leaf", None),
        P("leaf", "col", None, None, None),
        P("leaf", "col", None),
        P("leaf", "col", None),
        P("leaf", "col"),
    )
    out_specs = P(("leaf", "col"), None)
    return jax.shard_map(body, mesh=mesh, in_specs=in_specs, out_specs=out_specs, check_vma=False)
```

```python
import jax
import jax.numpy as jnp
from jax import lax
from jax.experimental import pallas as pl
from jax.experimental.pallas import tpu as pltpu
from jax.sharding import PartitionSpec as P

BLOCK = 128
ROW_BLOCKS = 16
LIST_LEN = 96
COLUMNS = 256
SLOTS = 14
ROWS = ROW_BLOCKS * BLOCK
WIDTH = SLOTS * BLOCK
Z = 8
X = 4
HALF = COLUMNS // 2
MESH = pl.DeviceIdType.MESH
GROUPS = 8
PER_GROUP = LIST_LEN // GROUPS
F32 = jnp.float32
BF16 = jnp.bfloat16


def build_kernel(row_hbm, col_hbm, count_ref, blocks_hbm, dense, block_buf, extra, row_ref, col_ref, seen, sems):
    lists = []
    for n, (source, target) in enumerate(((row_hbm, row_ref), (col_hbm, col_ref))):
        lists.append(pltpu.make_async_copy(source, target, sems.at[GROUPS + n]))
        lists[-1].start()
    fetches = []
    for g in range(GROUPS):
        part = pl.ds(g * PER_GROUP, PER_GROUP)
        fetches.append(pltpu.make_async_copy(blocks_hbm.at[0, 0, part], block_buf.at[part], sems.at[g]))
        fetches[-1].start()

    @pl.loop(0, ROW_BLOCKS)
    def _(i):
        for c in range(SLOTS):
            seen[i * SLOTS + c] = -1

    @pl.loop(0, ROWS // 64)
    def _(i):
        dense[pl.ds(pl.multiple_of(i * 64, 64), 64), :] = jnp.zeros((64, WIDTH), BF16)

    for c in lists:
        c.wait()
    count = count_ref[0, 0]
    used = jnp.int32(0)
    for g in range(GROUPS):
        fetches[g].wait()

        def add_block(k, used):
            r = row_ref[0, 0, k]
            c = col_ref[0, 0, k]
            place = r * SLOTS + c
            state = seen[place]
            rows = pl.ds(pl.multiple_of(r * BLOCK, BLOCK), BLOCK)
            cols = pl.ds(pl.multiple_of(c * BLOCK, BLOCK), BLOCK)

            @pl.when(state == -1)
            def _():
                dense[rows, cols] = block_buf[k]
                seen[place] = -2

            @pl.when(state == -2)
            def _():
                total = dense[rows, cols].astype(F32) + block_buf[k].astype(F32)
                extra[used] = total
                dense[rows, cols] = total.astype(BF16)
                seen[place] = used

            @pl.when(state >= 0)
            def _():
                total = extra[state] + block_buf[k].astype(F32)
                extra[state] = total
                dense[rows, cols] = total.astype(BF16)

            return used + jnp.where(state == -2, 1, 0)

        used = lax.fori_loop(g * PER_GROUP, jnp.clip(count, g * PER_GROUP, (g + 1) * PER_GROUP), add_block, used)


def level_lanes(level, levels=1):
    start = (2 + (level - 1) * 2) * BLOCK
    return slice(start, start + levels * 2 * BLOCK)


TOP = level_lanes(5, 2)
LATE = level_lanes(4, 3)
EARLY = slice(0, LATE.start)
COPIES = 96


def dot_t(a, b):
    return lax.dot_general(a, b, (((1,), (1,)), ((), ())), preferred_element_type=F32)


def solve_kernel(
    dense, right, out,
    right_t, coarse, pair_in, own, one_in, z_out, z_in, quad_in, next_in, x_out, x_in,
    terms, y_far, y_far_in, y_out, y_in, send, recv,
):
    leaf = lax.axis_index("leaf")
    col = lax.axis_index("col")
    core = lax.rem(leaf, 2)
    z = lax.rem(leaf // 2, Z)
    x = leaf // (2 * Z)
    quad = z // 4
    in_quad = lax.rem(z, 4)

    def at(x_to, z_to, core_to):
        return ((x_to * Z + z_to) * 2 + core_to, col)

    partner = at(x, z, 1 - core)
    z_peer = [at(x, lax.rem(z + d, Z), core) for d in range(Z)]
    quad_peer = [at(x, quad * 4 + lax.rem(in_quad + d, 4), core) for d in range(4)]
    z_next = z + 1 - 2 * lax.rem(z, 2)
    x_peer = []
    for b in range(X):
        flip_0 = x + 1 - 2 * lax.rem(x, 2) if b & 1 else x
        high = flip_0 // 2
        flip_1 = flip_0 + 2 - 4 * high if b & 2 else flip_0
        x_peer.append(at(flip_1, z, core))
    up = (leaf, lax.rem(col + 1, 4))
    down = (leaf, lax.rem(col + 3, 4))

    barrier = pltpu.get_barrier_semaphore()
    peers = [z_peer[d] for d in (4, 3, 5, 2, 6, 1, 7)] + x_peer[1:] + [up, down, partner]
    for peer in peers:
        pl.semaphore_signal(barrier, inc=1, device_id=peer, device_id_type=MESH)

    started = []

    def copy(src, dst, to):
        n = len(started)
        c = pltpu.make_async_remote_copy(
            src_ref=src, dst_ref=dst, send_sem=send.at[n], recv_sem=recv.at[n], device_id=to, device_id_type=MESH
        )
        c.start()
        started.append(c)
        return c

    def wait_all(copies):
        for c in copies:
            c.wait_recv()

    mine = pl.ds(pl.multiple_of(core * HALF, HALF), HALF)
    other = pl.ds(pl.multiple_of((1 - core) * HALF, HALF), HALF)
    chunk = pl.ds(pl.multiple_of(core * HALF + z * 16, 16), 16)
    quad_rows = pl.ds(pl.multiple_of(core * HALF + in_quad * 32, 32), 32)
    one, two, three, four = (level_lanes(level) for level in (1, 2, 3, 4))

    def partial(lanes):
        own[:, lanes] = lax.dot_general(
            right_t[...], dense[:, lanes], (((1,), (0,)), ((), ())), preferred_element_type=F32
        )

    def pair_send(lanes):
        return copy(own.at[other, lanes], pair_in.at[:, lanes], partner)

    def pair_sum(pair, lanes):
        pair.wait_recv()
        total = own[mine, lanes] + pair_in[:, lanes]
        own[mine, lanes] = total
        z_out[:, lanes] = total.astype(BF16)

    def ring_send(lanes):
        copies = []
        for d in (4, 3, 5, 2, 6, 1, 7):
            rows = pl.ds(pl.multiple_of(lax.rem(z + d, Z) * 16, 16), 16)
            copies.append(copy(z_out.at[rows, lanes], z_in.at[d, :, lanes], z_peer[d]))
        return copies

    def ring_sum(copies, lanes):
        wait_all(copies)
        total = own[chunk, lanes]
        for d in range(1, Z):
            total += z_in[d, :, lanes].astype(F32)
        return total

    def ring_share(lanes):
        return [copy(coarse.at[chunk, lanes], coarse.at[chunk, lanes], z_peer[d]) for d in (4, 3, 5, 2, 6, 1, 7)]

    def give(lanes):
        return copy(coarse.at[mine, lanes], coarse.at[mine, lanes], partner)

    @pl.loop(0, ROW_BLOCKS)
    def _(i):
        rows = pl.ds(pl.multiple_of(i * BLOCK, BLOCK), BLOCK)
        right_t[:, rows] = right[rows, :].T

    partial(TOP)
    pl.semaphore_wait(barrier, len(peers))
    top_pair = pair_send(TOP)
    partial(four)
    four_pair = pair_send(four)
    pair_sum(top_pair, TOP)
    top_ring = ring_send(TOP)
    pair_sum(four_pair, four)
    four_ring = ring_send(four)
    partial(three)
    three_pair = pair_send(three)
    partial(two)
    two_pair = pair_send(two)
    pair_sum(three_pair, three)
    three_quad = []
    for d in (2, 1, 3):
        rows = pl.ds(pl.multiple_of(lax.rem(in_quad + d, 4) * 32, 32), 32)
        three_quad.append(copy(z_out.at[rows, three], quad_in.at[d], quad_peer[d]))
    pair_sum(two_pair, two)
    two_next = copy(z_out.at[:, two], next_in, at(x, z_next, core))
    partial(slice(0, one.stop))
    one_pair = copy(own.at[:, one], one_in, partner)
    coarse[:, 0:one.start] = own[:, 0:one.start].astype(BF16)

    x_out[...] = ring_sum(top_ring, TOP)
    six = slice(2 * BLOCK, 4 * BLOCK)
    x_copies = [
        copy(x_out.at[:, six], x_in.at[2, :, six], x_peer[2]),
        copy(x_out, x_in.at[1], x_peer[1]),
        copy(x_out.at[:, six], x_in.at[3, :, six], x_peer[3]),
    ]

    coarse[chunk, four] = ring_sum(four_ring, four).astype(BF16)
    four_share = ring_share(four)
    wait_all(three_quad)
    total = own[quad_rows, three]
    for d in range(1, 4):
        total += quad_in[d].astype(F32)
    coarse[quad_rows, three] = total.astype(BF16)
    three_share = [copy(coarse.at[quad_rows, three], coarse.at[quad_rows, three], quad_peer[d]) for d in (2, 1, 3)]

    wait_all(x_copies)
    coarse[chunk, TOP.start:TOP.start + 2 * BLOCK] = (x_out[:, 0:2 * BLOCK] + x_in[1, :, 0:2 * BLOCK]).astype(BF16)
    coarse[chunk, TOP.start + 2 * BLOCK:TOP.stop] = (
        (x_out[:, six] + x_in[1, :, six]) + (x_in[2, :, six] + x_in[3, :, six])
    ).astype(BF16)
    top_share = ring_share(TOP)

    two_next.wait_recv()
    coarse[mine, two] = (own[mine, two] + next_in[...].astype(F32)).astype(BF16)
    two_give = give(two)
    one_pair.wait_recv()
    coarse[:, one] = (own[:, one] + one_in[...]).astype(BF16)
    wait_all(three_share)
    three_give = give(three)
    wait_all([two_give, three_give])

    @pl.loop(0, ROWS // 256)
    def _(i):
        rows = pl.ds(pl.multiple_of(i * 256, 256), 256)
        terms[rows, :] = dot_t(dense[rows, EARLY], coarse[:, EARLY])

    wait_all(four_share)
    four_give = give(four)
    wait_all(top_share)
    top_give = give(TOP)
    wait_all([four_give, top_give])

    def finish(quarter, half):
        rows = pl.ds(pl.multiple_of(quarter * 512 + half * 256, 256), 256)
        return terms[rows, :] + dot_t(dense[rows, LATE], coarse[:, LATE])

    far = lax.rem(col + 2, 4)
    above = lax.rem(col + 1, 4)
    below = lax.rem(col + 3, 4)
    far_copies = []
    for way, to in ((0, up), (1, down)):
        y_far[way] = finish(far, way).astype(BF16)
        for piece in range(2):
            rows = pl.ds(piece * BLOCK, BLOCK)
            far_copies.append(copy(y_far.at[way, rows], y_far_in.at[way, rows], to))
    y_out[0, 1] = finish(above, 1).astype(BF16)
    up_direct = copy(y_out.at[0, 1], y_in.at[0, 1], up)
    y_out[1, 0] = finish(below, 0).astype(BF16)
    down_direct = copy(y_out.at[1, 0], y_in.at[1, 0], down)
    passing = (finish(above, 0), finish(below, 1))
    for way, quarter in ((0, above), (1, below)):
        rows = pl.ds(pl.multiple_of(quarter * 512 + way * 256, 256), 256)
        terms[rows, :] = passing[way]
    last = []
    for piece in range(2):
        for way, quarter, to in ((0, above, up), (1, below, down)):
            far_copies[way * 2 + piece].wait_recv()
            rows = pl.ds(piece * BLOCK, BLOCK)
            from_terms = pl.ds(pl.multiple_of(quarter * 512 + way * 256 + piece * BLOCK, BLOCK), BLOCK)
            y_out[way, way, rows] = (terms[from_terms, :] + y_far_in[way, rows].astype(F32)).astype(BF16)
            last.append(copy(y_out.at[way, way, rows], y_in.at[way, way, rows], to))
    for half in range(2):
        rows = pl.ds(pl.multiple_of(col * 512 + half * 256, 256), 256)
        terms[rows, :] = finish(col, half)
    wait_all([up_direct, down_direct] + last)
    for half in range(2):
        rows = pl.ds(pl.multiple_of(col * 512 + half * 256, 256), 256)
        total = terms[rows, :] + (y_in[0, half].astype(F32) + y_in[1, half].astype(F32))
        out[half * 256:(half + 1) * 256, :] = total.astype(BF16)
    for c in started:
        c.wait_send()


def stay(array):
    return pltpu.with_memory_space_constraint(array, pltpu.HBM)


def body(right_side, x_blocks, row_ids, col_ids, counts):
    vmem = pl.BlockSpec(memory_space=pltpu.VMEM)
    hbm = pl.BlockSpec(memory_space=pltpu.HBM)
    dense = pl.pallas_call(
        build_kernel,
        out_shape=jax.ShapeDtypeStruct((ROWS, WIDTH), BF16),
        in_specs=[hbm, hbm, pl.BlockSpec(memory_space=pltpu.SMEM), hbm],
        out_specs=vmem,
        scratch_shapes=[
            pltpu.VMEM((LIST_LEN, BLOCK, BLOCK), BF16),
            pltpu.VMEM((LIST_LEN // 2, BLOCK, BLOCK), F32),
            pltpu.SMEM((1, 1, LIST_LEN), jnp.int32),
            pltpu.SMEM((1, 1, LIST_LEN), jnp.int32),
            pltpu.SMEM((ROW_BLOCKS * SLOTS,), jnp.int32),
            pltpu.SemaphoreType.DMA((GROUPS + 2,)),
        ],
        compiler_params=pltpu.CompilerParams(vmem_limit_bytes=24 * 2**20),
        name="build_dense",
    )(stay(row_ids), stay(col_ids), counts, stay(x_blocks))
    return pl.pallas_call(
        solve_kernel,
        out_shape=jax.ShapeDtypeStruct((ROWS // 4, COLUMNS), BF16),
        in_specs=[vmem, vmem],
        out_specs=vmem,
        scratch_shapes=[
            pltpu.VMEM((COLUMNS, ROWS), BF16),
            pltpu.VMEM((COLUMNS, WIDTH), BF16),
            pltpu.VMEM((HALF, WIDTH), F32),
            pltpu.VMEM((COLUMNS, WIDTH), F32),
            pltpu.VMEM((COLUMNS, 2 * BLOCK), F32),
            pltpu.VMEM((HALF, WIDTH), BF16),
            pltpu.VMEM((Z, 16, WIDTH), BF16),
            pltpu.VMEM((4, 32, 2 * BLOCK), BF16),
            pltpu.VMEM((HALF, 2 * BLOCK), BF16),
            pltpu.VMEM((16, 4 * BLOCK), F32),
            pltpu.VMEM((X, 16, 4 * BLOCK), F32),
            pltpu.VMEM((ROWS, COLUMNS), F32),
            pltpu.VMEM((2, 256, COLUMNS), BF16),
            pltpu.VMEM((2, 256, COLUMNS), BF16),
            pltpu.VMEM((2, 2, 256, COLUMNS), BF16),
            pltpu.VMEM((2, 2, 256, COLUMNS), BF16),
            pltpu.SemaphoreType.DMA((COPIES,)),
            pltpu.SemaphoreType.DMA((COPIES,)),
        ],
        compiler_params=pltpu.CompilerParams(
            collective_id=0, has_side_effects=True, vmem_limit_bytes=32 * 2**20
        ),
        name="solve",
    )(dense, right_side)


def solution(mesh):
    in_specs = (
        P("leaf", None),
        P("leaf", "col", None, None, None),
        P("leaf", "col", None),
        P("leaf", "col", None),
        P("leaf", "col"),
    )
    out_specs = P(("leaf", "col"), None)
    return jax.shard_map(body, mesh=mesh, in_specs=in_specs, out_specs=out_specs, check_vma=False)
```

```python
import jax
import jax.numpy as jnp
from jax import lax
from jax.experimental import pallas as pl
from jax.experimental.pallas import tpu as pltpu
from jax.sharding import PartitionSpec as P

BLOCK = 128
ROW_BLOCKS = 16
LIST_LEN = 96
COLUMNS = 256
SLOTS = 14
ROWS = ROW_BLOCKS * BLOCK
WIDTH = SLOTS * BLOCK
Z = 8
X = 4
HALF = COLUMNS // 2
MESH = pl.DeviceIdType.MESH
GROUPS = 8
PER_GROUP = LIST_LEN // GROUPS
F32 = jnp.float32
BF16 = jnp.bfloat16


def lane_block(slot):
    level = slot // 2
    side = lax.rem(slot, 2)
    late = 8 + side * 3 + (level - 4)
    mid = 4 + side * 2 + (level - 2)
    return jnp.where(slot >= 8, late, jnp.where(slot >= 4, mid, slot))


def build_kernel(row_hbm, col_hbm, count_ref, blocks_hbm, dense, block_buf, extra, row_ref, col_ref, seen, sems):
    lists = []
    for n, (source, target) in enumerate(((row_hbm, row_ref), (col_hbm, col_ref))):
        lists.append(pltpu.make_async_copy(source, target, sems.at[GROUPS + n]))
        lists[-1].start()
    fetches = []
    for g in range(GROUPS):
        part = pl.ds(g * PER_GROUP, PER_GROUP)
        fetches.append(pltpu.make_async_copy(blocks_hbm.at[0, 0, part], block_buf.at[part], sems.at[g]))
        fetches[-1].start()

    @pl.loop(0, ROW_BLOCKS)
    def _(i):
        for c in range(SLOTS):
            seen[i * SLOTS + c] = -1

    @pl.loop(0, ROWS // 64)
    def _(i):
        dense[pl.ds(pl.multiple_of(i * 64, 64), 64), :] = jnp.zeros((64, WIDTH), BF16)

    for c in lists:
        c.wait()
    count = count_ref[0, 0]
    used = jnp.int32(0)
    for g in range(GROUPS):
        fetches[g].wait()

        def add_block(k, used):
            r = row_ref[0, 0, k]
            c = lane_block(col_ref[0, 0, k])
            place = r * SLOTS + c
            state = seen[place]
            rows = pl.ds(pl.multiple_of(r * BLOCK, BLOCK), BLOCK)
            cols = pl.ds(pl.multiple_of(c * BLOCK, BLOCK), BLOCK)

            @pl.when(state == -1)
            def _():
                dense[rows, cols] = block_buf[k]
                seen[place] = -2

            @pl.when(state == -2)
            def _():
                total = dense[rows, cols].astype(F32) + block_buf[k].astype(F32)
                extra[used] = total
                dense[rows, cols] = total.astype(BF16)
                seen[place] = used

            @pl.when(state >= 0)
            def _():
                total = extra[state] + block_buf[k].astype(F32)
                extra[state] = total
                dense[rows, cols] = total.astype(BF16)

            return used + jnp.where(state == -2, 1, 0)

        used = lax.fori_loop(g * PER_GROUP, jnp.clip(count, g * PER_GROUP, (g + 1) * PER_GROUP), add_block, used)


INNER = slice(0, 2 * BLOCK)
ONE = slice(2 * BLOCK, 4 * BLOCK)
MID = slice(4 * BLOCK, 8 * BLOCK)
LATE = slice(8 * BLOCK, 14 * BLOCK)
RING_ORDER = (4, 3, 5, 2, 6, 1, 7)
COPIES = 80


def dot_t(a, b):
    return lax.dot_general(a, b, (((1,), (1,)), ((), ())), preferred_element_type=F32)


def solve_kernel(
    dense, right, out,
    right_t, coarse, own, late_in, mid_in, one_in, late_out, mid_out, ring_in, quad_in, next_in, x_out, x_in,
    terms, y_far, y_far_in, y_out, y_in, send, recv,
):
    leaf = lax.axis_index("leaf")
    col = lax.axis_index("col")
    core = lax.rem(leaf, 2)
    z = lax.rem(leaf // 2, Z)
    x = leaf // (2 * Z)
    quad = z // 4
    in_quad = lax.rem(z, 4)

    def at(x_to, z_to, core_to):
        return ((x_to * Z + z_to) * 2 + core_to, col)

    partner = at(x, z, 1 - core)
    z_peer = [at(x, lax.rem(z + d, Z), core) for d in range(Z)]
    quad_peer = [at(x, quad * 4 + lax.rem(in_quad + d, 4), core) for d in range(4)]
    z_next = at(x, z + 1 - 2 * lax.rem(z, 2), core)
    x_peer = []
    for b in range(X):
        flip_0 = x + 1 - 2 * lax.rem(x, 2) if b & 1 else x
        high = flip_0 // 2
        flip_1 = flip_0 + 2 - 4 * high if b & 2 else flip_0
        x_peer.append(at(flip_1, z, core))
    up = (leaf, lax.rem(col + 1, 4))
    down = (leaf, lax.rem(col + 3, 4))

    barrier = pltpu.get_barrier_semaphore()
    peers = [z_peer[d] for d in RING_ORDER] + x_peer[1:] + [up, down, partner]
    for peer in peers:
        pl.semaphore_signal(barrier, inc=1, device_id=peer, device_id_type=MESH)

    started = []

    def copy(src, dst, to):
        n = len(started)
        c = pltpu.make_async_remote_copy(
            src_ref=src, dst_ref=dst, send_sem=send.at[n], recv_sem=recv.at[n], device_id=to, device_id_type=MESH
        )
        c.start()
        started.append(c)
        return c

    def wait_all(copies):
        for c in copies:
            c.wait_recv()

    late_mine = pl.ds(pl.multiple_of(LATE.start + core * 384, BLOCK), 384)
    late_other = pl.ds(pl.multiple_of(LATE.start + (1 - core) * 384, BLOCK), 384)
    mid_mine = pl.ds(pl.multiple_of(MID.start + core * 256, BLOCK), 256)
    mid_other = pl.ds(pl.multiple_of(MID.start + (1 - core) * 256, BLOCK), 256)
    two_mine = pl.ds(pl.multiple_of(MID.start + core * 256, BLOCK), BLOCK)
    three_mine = pl.ds(pl.multiple_of(MID.start + core * 256 + BLOCK, BLOCK), BLOCK)
    four_mine = pl.ds(pl.multiple_of(LATE.start + core * 384, BLOCK), BLOCK)
    five_mine = pl.ds(pl.multiple_of(LATE.start + core * 384 + BLOCK, BLOCK), BLOCK)
    six_mine = pl.ds(pl.multiple_of(LATE.start + core * 384 + 2 * BLOCK, BLOCK), BLOCK)
    part_rows = [pl.ds(p * HALF, HALF) for p in range(2)]
    chunk = [pl.ds(pl.multiple_of(p * HALF + z * 16, 16), 16) for p in range(2)]
    quad_chunk = [pl.ds(pl.multiple_of(p * HALF + in_quad * 32, 32), 32) for p in range(2)]

    def partial(lanes):
        own[:, lanes] = lax.dot_general(
            right_t[...], dense[:, lanes], (((1,), (0,)), ((), ())), preferred_element_type=F32
        )

    @pl.loop(0, ROW_BLOCKS)
    def _(i):
        rows = pl.ds(pl.multiple_of(i * BLOCK, BLOCK), BLOCK)
        right_t[:, rows] = right[rows, :].T

    partial(LATE)
    pl.semaphore_wait(barrier, len(peers))
    late_pair = [copy(own.at[part_rows[p], late_other], late_in.at[part_rows[p]], partner) for p in range(2)]
    partial(MID)
    mid_pair = [copy(own.at[part_rows[p], mid_other], mid_in.at[part_rows[p]], partner) for p in range(2)]

    late_ring = []
    for p in range(2):
        late_pair[p].wait_recv()
        total = own[part_rows[p], late_mine] + late_in[part_rows[p]]
        own[part_rows[p], late_mine] = total
        late_out[part_rows[p]] = total.astype(BF16)
        ring = []
        for d in RING_ORDER:
            rows = pl.ds(pl.multiple_of(p * HALF + lax.rem(z + d, Z) * 16, 16), 16)
            ring.append(copy(late_out.at[rows], ring_in.at[p, d], z_peer[d]))
        late_ring.append(ring)
    mid_quad = []
    mid_next = []
    for p in range(2):
        mid_pair[p].wait_recv()
        total = own[part_rows[p], mid_mine] + mid_in[part_rows[p]]
        own[part_rows[p], mid_mine] = total
        mid_out[part_rows[p]] = total.astype(BF16)
        quads = []
        for d in (2, 1, 3):
            rows = pl.ds(pl.multiple_of(p * HALF + lax.rem(in_quad + d, 4) * 32, 32), 32)
            quads.append(copy(mid_out.at[rows, BLOCK:2 * BLOCK], quad_in.at[p, d], quad_peer[d]))
        mid_quad.append(quads)
        mid_next.append(copy(mid_out.at[part_rows[p], 0:BLOCK], next_in.at[part_rows[p]], z_next))
    partial(ONE)
    one_pair = copy(own.at[:, ONE], one_in, partner)
    partial(INNER)
    coarse[:, INNER] = own[:, INNER].astype(BF16)

    x_copies = []
    for p in range(2):
        wait_all(late_ring[p])
        total = own[chunk[p], late_mine]
        for d in range(1, Z):
            total += ring_in[p, d].astype(F32)
        coarse[chunk[p], four_mine] = total[:, 0:BLOCK].astype(BF16)
        x_out[p] = total[:, BLOCK:3 * BLOCK]
        x_copies.append([
            copy(x_out.at[p, :, BLOCK:2 * BLOCK], x_in.at[p, 2, :, BLOCK:2 * BLOCK], x_peer[2]),
            copy(x_out.at[p], x_in.at[p, 1], x_peer[1]),
            copy(x_out.at[p, :, BLOCK:2 * BLOCK], x_in.at[p, 3, :, BLOCK:2 * BLOCK], x_peer[3]),
        ])
    late_share = []
    mid_share = []
    for p in range(2):
        wait_all(mid_quad[p])
        total = own[quad_chunk[p], three_mine]
        for d in range(1, 4):
            total += quad_in[p, d].astype(F32)
        coarse[quad_chunk[p], three_mine] = total.astype(BF16)
        at_three = coarse.at[quad_chunk[p], three_mine]
        mid_share.append([copy(at_three, at_three, quad_peer[d]) for d in (2, 1, 3)])
        wait_all(x_copies[p])
        coarse[chunk[p], five_mine] = (x_out[p, :, 0:BLOCK] + x_in[p, 1, :, 0:BLOCK]).astype(BF16)
        coarse[chunk[p], six_mine] = (
            (x_out[p, :, BLOCK:2 * BLOCK] + x_in[p, 1, :, BLOCK:2 * BLOCK])
            + (x_in[p, 2, :, BLOCK:2 * BLOCK] + x_in[p, 3, :, BLOCK:2 * BLOCK])
        ).astype(BF16)
        at_late = coarse.at[chunk[p], late_mine]
        late_share.append([copy(at_late, at_late, z_peer[d]) for d in RING_ORDER])
    one_pair.wait_recv()
    coarse[:, ONE] = (own[:, ONE] + one_in[...]).astype(BF16)

    @pl.loop(0, ROWS // 256)
    def _(i):
        rows = pl.ds(pl.multiple_of(i * 256, 256), 256)
        terms[rows, :] = dot_t(dense[rows, 0:ONE.stop], coarse[:, 0:ONE.stop])


    def give_part(p):
        mid_next[p].wait_recv()
        coarse[part_rows[p], two_mine] = (own[part_rows[p], two_mine] + next_in[part_rows[p]].astype(F32)).astype(BF16)
        wait_all(mid_share[p])
        at_mid = coarse.at[part_rows[p], mid_mine]
        gives = [copy(at_mid, at_mid, partner)]
        wait_all(late_share[p])
        at_late = coarse.at[part_rows[p], late_mine]
        gives.append(copy(at_late, at_late, partner))
        wait_all(gives)

    def finish(p, quarter, half):
        rows = pl.ds(pl.multiple_of(quarter * 512 + half * 256, 256), 256)
        return terms[rows, p * HALF:(p + 1) * HALF] + dot_t(dense[rows, MID.start:WIDTH], coarse[part_rows[p], MID.start:WIDTH])

    far = lax.rem(col + 2, 4)
    nearby = (lax.rem(col + 1, 4), lax.rem(col + 3, 4))
    toward = (up, down)

    def send_far(p):
        copies = []
        for way in range(2):
            y_far[p, way] = finish(p, far, way).astype(BF16)
            copies.append(copy(y_far.at[p, way], y_far_in.at[p, way], toward[way]))
        return copies

    def send_direct(p):
        copies = []
        for way in range(2):
            y_out[p, way, 1 - way] = finish(p, nearby[way], 1 - way).astype(BF16)
            copies.append(copy(y_out.at[p, way, 1 - way], y_in.at[p, way, 1 - way], toward[way]))
        return copies

    def send_passed(p, far_copies):
        copies = []
        for way in range(2):
            value = finish(p, nearby[way], way)
            far_copies[way].wait_recv()
            y_out[p, way, way] = (value + y_far_in[p, way].astype(F32)).astype(BF16)
            copies.append(copy(y_out.at[p, way, way], y_in.at[p, way, way], toward[way]))
        return copies

    give_part(0)
    far_a = send_far(0)
    last = send_direct(0)
    give_part(1)
    far_b = send_far(1)
    last += send_passed(0, far_a)
    last += send_direct(1)
    last += send_passed(1, far_b)
    for p in range(2):
        for half in range(2):
            rows = pl.ds(pl.multiple_of(col * 512 + half * 256, 256), 256)
            terms[rows, p * HALF:(p + 1) * HALF] = finish(p, col, half)
    wait_all(last)
    for p in range(2):
        for half in range(2):
            rows = pl.ds(pl.multiple_of(col * 512 + half * 256, 256), 256)
            total = terms[rows, p * HALF:(p + 1) * HALF] + (y_in[p, 0, half].astype(F32) + y_in[p, 1, half].astype(F32))
            out[half * 256:(half + 1) * 256, p * HALF:(p + 1) * HALF] = total.astype(BF16)
    for c in started:
        c.wait_send()


def stay(array):
    return pltpu.with_memory_space_constraint(array, pltpu.HBM)


def body(right_side, x_blocks, row_ids, col_ids, counts):
    vmem = pl.BlockSpec(memory_space=pltpu.VMEM)
    hbm = pl.BlockSpec(memory_space=pltpu.HBM)
    dense = pl.pallas_call(
        build_kernel,
        out_shape=jax.ShapeDtypeStruct((ROWS, WIDTH), BF16),
        in_specs=[hbm, hbm, pl.BlockSpec(memory_space=pltpu.SMEM), hbm],
        out_specs=vmem,
        scratch_shapes=[
            pltpu.VMEM((LIST_LEN, BLOCK, BLOCK), BF16),
            pltpu.VMEM((LIST_LEN // 2, BLOCK, BLOCK), F32),
            pltpu.SMEM((1, 1, LIST_LEN), jnp.int32),
            pltpu.SMEM((1, 1, LIST_LEN), jnp.int32),
            pltpu.SMEM((ROW_BLOCKS * SLOTS,), jnp.int32),
            pltpu.SemaphoreType.DMA((GROUPS + 2,)),
        ],
        compiler_params=pltpu.CompilerParams(vmem_limit_bytes=24 * 2**20),
        name="build_dense",
    )(stay(row_ids), stay(col_ids), counts, stay(x_blocks))
    return pl.pallas_call(
        solve_kernel,
        out_shape=jax.ShapeDtypeStruct((ROWS // 4, COLUMNS), BF16),
        in_specs=[vmem, vmem],
        out_specs=vmem,
        scratch_shapes=[
            pltpu.VMEM((COLUMNS, ROWS), BF16),
            pltpu.VMEM((COLUMNS, WIDTH), BF16),
            pltpu.VMEM((COLUMNS, WIDTH), F32),
            pltpu.VMEM((COLUMNS, 3 * BLOCK), F32),
            pltpu.VMEM((COLUMNS, 2 * BLOCK), F32),
            pltpu.VMEM((COLUMNS, 2 * BLOCK), F32),
            pltpu.VMEM((COLUMNS, 3 * BLOCK), BF16),
            pltpu.VMEM((COLUMNS, 2 * BLOCK), BF16),
            pltpu.VMEM((2, Z, 16, 3 * BLOCK), BF16),
            pltpu.VMEM((2, 4, 32, BLOCK), BF16),
            pltpu.VMEM((COLUMNS, BLOCK), BF16),
            pltpu.VMEM((2, 16, 2 * BLOCK), F32),
            pltpu.VMEM((2, X, 16, 2 * BLOCK), F32),
            pltpu.VMEM((ROWS, COLUMNS), F32),
            pltpu.VMEM((2, 2, 256, HALF), BF16),
            pltpu.VMEM((2, 2, 256, HALF), BF16),
            pltpu.VMEM((2, 2, 2, 256, HALF), BF16),
            pltpu.VMEM((2, 2, 2, 256, HALF), BF16),
            pltpu.SemaphoreType.DMA((COPIES,)),
            pltpu.SemaphoreType.DMA((COPIES,)),
        ],
        compiler_params=pltpu.CompilerParams(
            collective_id=0, has_side_effects=True, vmem_limit_bytes=32 * 2**20
        ),
        name="solve",
    )(dense, right_side)


def solution(mesh):
    in_specs = (
        P("leaf", None),
        P("leaf", "col", None, None, None),
        P("leaf", "col", None),
        P("leaf", "col", None),
        P("leaf", "col"),
    )
    out_specs = P(("leaf", "col"), None)
    return jax.shard_map(body, mesh=mesh, in_specs=in_specs, out_specs=out_specs, check_vma=False)
```

```python
import jax
import jax.numpy as jnp
from jax import lax
from jax.experimental import pallas as pl
from jax.experimental.pallas import tpu as pltpu
from jax.sharding import PartitionSpec as P

BLOCK = 128
ROW_BLOCKS = 16
LIST_LEN = 96
COLUMNS = 256
SLOTS = 14
ROWS = ROW_BLOCKS * BLOCK
WIDTH = SLOTS * BLOCK
Z = 8
X = 4
HALF = COLUMNS // 2
MESH = pl.DeviceIdType.MESH
GROUPS = 8
PER_GROUP = LIST_LEN // GROUPS
F32 = jnp.float32
BF16 = jnp.bfloat16


def lane_block(slot):
    level = slot // 2
    side = lax.rem(slot, 2)
    late = 8 + side * 3 + (level - 4)
    mid = 4 + side * 2 + (level - 2)
    return jnp.where(slot >= 8, late, jnp.where(slot >= 4, mid, slot))


def build_kernel(
    row_hbm, col_hbm, count_ref, right_hbm, blocks_hbm, dense, right_t,
    right_buf, block_buf, extra, row_ref, col_ref, row_at, col_at, seen, slot_of, again, first, sems,
):
    lists = []
    for n, (source, target) in enumerate(((row_hbm, row_ref), (col_hbm, col_ref))):
        lists.append(pltpu.make_async_copy(source, target, sems.at[GROUPS + n]))
        lists[-1].start()
    fetch_right = pltpu.make_async_copy(right_hbm, right_buf, sems.at[GROUPS + 2])
    fetch_right.start()
    fetches = []
    for g in range(GROUPS):
        part = pl.ds(g * PER_GROUP, PER_GROUP)
        fetches.append(pltpu.make_async_copy(blocks_hbm.at[0, 0, part], block_buf.at[part], sems.at[g]))
        fetches[-1].start()

    @pl.loop(0, ROW_BLOCKS)
    def _(i):
        for c in range(SLOTS):
            seen[i * SLOTS + c] = -1

    @pl.loop(0, ROWS // 64)
    def _(i):
        dense[pl.ds(pl.multiple_of(i * 64, 64), 64), :] = jnp.zeros((64, WIDTH), BF16)

    for c in lists:
        c.wait()
    count = count_ref[0, 0]

    def place_block(k, repeats):
        r = row_ref[0, 0, k]
        c = lane_block(col_ref[0, 0, k])
        row_at[k] = r * BLOCK
        col_at[k] = c * BLOCK
        slot_of[k] = -1
        place = r * SLOTS + c
        earlier = seen[place]
        again[repeats] = k
        first[repeats] = earlier
        seen[place] = jnp.where(earlier >= 0, earlier, k)
        return repeats + jnp.where(earlier >= 0, 1, 0)

    repeats = lax.fori_loop(0, count, place_block, jnp.int32(0))
    fetch_right.wait()

    @pl.loop(0, ROW_BLOCKS)
    def _(i):
        rows = pl.ds(pl.multiple_of(i * BLOCK, BLOCK), BLOCK)
        right_t[:, rows] = right_buf[rows, :].T

    def target(k):
        return pl.ds(pl.multiple_of(row_at[k], BLOCK), BLOCK), pl.ds(pl.multiple_of(col_at[k], BLOCK), BLOCK)

    for g in range(GROUPS):
        fetches[g].wait()

        @pl.when(g * PER_GROUP < count)
        def _():
            @pl.loop(0, PER_GROUP // 4)
            def _(i):
                for n in range(4):
                    k = jnp.minimum(g * PER_GROUP + i * 4 + n, count - 1)
                    rows, cols = target(k)
                    dense[rows, cols] = block_buf[k]

    def add_again(i, used):
        k = again[i]
        f = first[i]
        rows, cols = target(k)
        slot = slot_of[f]

        @pl.when(slot < 0)
        def _():
            total = block_buf[f].astype(F32) + block_buf[k].astype(F32)
            extra[used] = total
            dense[rows, cols] = total.astype(BF16)
            slot_of[f] = used

        @pl.when(slot >= 0)
        def _():
            total = extra[slot] + block_buf[k].astype(F32)
            extra[slot] = total
            dense[rows, cols] = total.astype(BF16)

        return used + jnp.where(slot < 0, 1, 0)

    lax.fori_loop(0, repeats, add_again, jnp.int32(0))


INNER = slice(0, 2 * BLOCK)
ONE = slice(2 * BLOCK, 4 * BLOCK)
MID = slice(4 * BLOCK, 8 * BLOCK)
LATE = slice(8 * BLOCK, 14 * BLOCK)
RING_ORDER = (4, 3, 5, 2, 6, 1, 7)
COPIES = 80


def dot_t(a, b):
    return lax.dot_general(a, b, (((1,), (1,)), ((), ())), preferred_element_type=F32)


def solve_kernel(
    dense, right_t, out,
    coarse_low, coarse_mid, coarse_late, own_one, own_mid, own_late, late_send, late_in, mid_in, one_in, late_out, mid_out,
    ring_in, quad_in, next_in, x_out, x_in,
    terms, y_far, y_far_in, y_out, y_in, send, recv,
):
    leaf = lax.axis_index("leaf")
    col = lax.axis_index("col")
    core = lax.rem(leaf, 2)
    z = lax.rem(leaf // 2, Z)
    x = leaf // (2 * Z)
    quad = z // 4
    in_quad = lax.rem(z, 4)

    def at(x_to, z_to, core_to):
        return ((x_to * Z + z_to) * 2 + core_to, col)

    partner = at(x, z, 1 - core)
    z_peer = [at(x, lax.rem(z + d, Z), core) for d in range(Z)]
    quad_peer = [at(x, quad * 4 + lax.rem(in_quad + d, 4), core) for d in range(4)]
    z_next = at(x, z + 1 - 2 * lax.rem(z, 2), core)
    x_peer = []
    for b in range(X):
        flip_0 = x + 1 - 2 * lax.rem(x, 2) if b & 1 else x
        high = flip_0 // 2
        flip_1 = flip_0 + 2 - 4 * high if b & 2 else flip_0
        x_peer.append(at(flip_1, z, core))
    up = (leaf, lax.rem(col + 1, 4))
    down = (leaf, lax.rem(col + 3, 4))

    barrier = pltpu.get_barrier_semaphore()
    peers = [z_peer[d] for d in RING_ORDER] + x_peer[1:] + [up, down, partner]
    for peer in peers:
        pl.semaphore_signal(barrier, inc=1, device_id=peer, device_id_type=MESH)

    started = []

    def copy(src, dst, to):
        n = len(started)
        c = pltpu.make_async_remote_copy(
            src_ref=src, dst_ref=dst, send_sem=send.at[n], recv_sem=recv.at[n], device_id=to, device_id_type=MESH
        )
        c.start()
        started.append(c)
        return c

    def wait_all(copies):
        for c in copies:
            c.wait_recv()

    part_rows = [pl.ds(p * HALF, HALF) for p in range(2)]
    chunk = [pl.ds(pl.multiple_of(p * HALF + z * 16, 16), 16) for p in range(2)]
    quad_chunk = [pl.ds(pl.multiple_of(p * HALF + in_quad * 32, 32), 32) for p in range(2)]

    def partial(lanes):
        return lax.dot_general(right_t[...], dense[:, lanes], (((1,), (0,)), ((), ())), preferred_element_type=F32)

    def late_lanes(side):
        return pl.ds(pl.multiple_of(LATE.start + side * 384, BLOCK), 384)

    late_send[...] = partial(late_lanes(1 - core))
    pl.semaphore_wait(barrier, len(peers))
    late_pair = [copy(late_send.at[part_rows[p]], late_in.at[part_rows[p]], partner) for p in range(2)]
    own_late[...] = partial(late_lanes(core))

    late_ring = []
    for p in range(2):
        late_pair[p].wait_recv()
        total = own_late[part_rows[p]] + late_in[part_rows[p]]
        own_late[part_rows[p]] = total
        late_out[part_rows[p]] = total.astype(BF16)
        ring = []
        for d in RING_ORDER:
            rows = pl.ds(pl.multiple_of(p * HALF + lax.rem(z + d, Z) * 16, 16), 16)
            ring.append(copy(late_out.at[rows], ring_in.at[p, d], z_peer[d]))
        late_ring.append(ring)
    value = partial(MID)
    for side in range(2):
        for n in range(2):
            own_mid[side, n] = value[:, (side * 2 + n) * BLOCK:(side * 2 + n + 1) * BLOCK]
    mid_pair = [copy(own_mid.at[1 - core, :, part_rows[p]], mid_in.at[:, part_rows[p]], partner) for p in range(2)]
    mid_quad = []
    mid_next = []
    for p in range(2):
        mid_pair[p].wait_recv()
        total = own_mid[core, :, part_rows[p]] + mid_in[:, part_rows[p]]
        own_mid[core, :, part_rows[p]] = total
        mid_out[:, part_rows[p]] = total.astype(BF16)
        quads = []
        for d in (2, 1, 3):
            rows = pl.ds(pl.multiple_of(p * HALF + lax.rem(in_quad + d, 4) * 32, 32), 32)
            quads.append(copy(mid_out.at[1, rows], quad_in.at[p, d], quad_peer[d]))
        mid_quad.append(quads)
        mid_next.append(copy(mid_out.at[0, part_rows[p]], next_in.at[part_rows[p]], z_next))
    own_one[...] = partial(ONE)
    one_pair = copy(own_one, one_in, partner)
    coarse_low[:, INNER] = partial(INNER).astype(BF16)

    x_copies = []
    for p in range(2):
        wait_all(late_ring[p])
        total = own_late[chunk[p]]
        for d in range(1, Z):
            total += ring_in[p, d].astype(F32)
        coarse_late[core, chunk[p], 0:BLOCK] = total[:, 0:BLOCK].astype(BF16)
        x_out[p] = total[:, BLOCK:3 * BLOCK]
        x_copies.append([
            copy(x_out.at[p, :, BLOCK:2 * BLOCK], x_in.at[p, 2, :, BLOCK:2 * BLOCK], x_peer[2]),
            copy(x_out.at[p], x_in.at[p, 1], x_peer[1]),
            copy(x_out.at[p, :, BLOCK:2 * BLOCK], x_in.at[p, 3, :, BLOCK:2 * BLOCK], x_peer[3]),
        ])
    late_share = []
    mid_share = []
    for p in range(2):
        wait_all(mid_quad[p])
        total = own_mid[core, 1, quad_chunk[p]]
        for d in range(1, 4):
            total += quad_in[p, d].astype(F32)
        coarse_mid[core, 1, quad_chunk[p]] = total.astype(BF16)
        at_three = coarse_mid.at[core, 1, quad_chunk[p]]
        mid_share.append([copy(at_three, at_three, quad_peer[d]) for d in (2, 1, 3)])
        wait_all(x_copies[p])
        coarse_late[core, chunk[p], BLOCK:2 * BLOCK] = (x_out[p, :, 0:BLOCK] + x_in[p, 1, :, 0:BLOCK]).astype(BF16)
        coarse_late[core, chunk[p], 2 * BLOCK:3 * BLOCK] = (
            (x_out[p, :, BLOCK:2 * BLOCK] + x_in[p, 1, :, BLOCK:2 * BLOCK])
            + (x_in[p, 2, :, BLOCK:2 * BLOCK] + x_in[p, 3, :, BLOCK:2 * BLOCK])
        ).astype(BF16)
        at_late = coarse_late.at[core, chunk[p]]
        late_share.append([copy(at_late, at_late, z_peer[d]) for d in RING_ORDER])
    one_pair.wait_recv()
    coarse_low[:, ONE] = (own_one[...] + one_in[...]).astype(BF16)

    @pl.loop(0, ROWS // 256)
    def _(i):
        rows = pl.ds(pl.multiple_of(i * 256, 256), 256)
        terms[rows, :] = dot_t(dense[rows, 0:ONE.stop], coarse_low[...])


    def give_part(p):
        mid_next[p].wait_recv()
        coarse_mid[core, 0, part_rows[p]] = (own_mid[core, 0, part_rows[p]] + next_in[part_rows[p]].astype(F32)).astype(BF16)
        wait_all(mid_share[p])
        at_mid = coarse_mid.at[core, :, part_rows[p]]
        gives = [copy(at_mid, at_mid, partner)]
        wait_all(late_share[p])
        at_late = coarse_late.at[core, part_rows[p]]
        gives.append(copy(at_late, at_late, partner))
        wait_all(gives)

    def finish(p, quarter, half):
        rows = pl.ds(pl.multiple_of(quarter * 512 + half * 256, 256), 256)
        pieces = [coarse_mid[side, n, part_rows[p]] for side in range(2) for n in range(2)]
        pieces += [coarse_late[side, part_rows[p]] for side in range(2)]
        coarse = jnp.concatenate(pieces, axis=1)
        return terms[rows, p * HALF:(p + 1) * HALF] + dot_t(dense[rows, MID.start:WIDTH], coarse)

    far = lax.rem(col + 2, 4)
    nearby = (lax.rem(col + 1, 4), lax.rem(col + 3, 4))
    toward = (up, down)

    def send_far(p):
        copies = []
        for way in range(2):
            y_far[p, way] = finish(p, far, way).astype(BF16)
            copies.append(copy(y_far.at[p, way], y_far_in.at[p, way], toward[way]))
        return copies

    def send_direct(p):
        copies = []
        for way in range(2):
            y_out[p, way, 1 - way] = finish(p, nearby[way], 1 - way).astype(BF16)
            copies.append(copy(y_out.at[p, way, 1 - way], y_in.at[p, way, 1 - way], toward[way]))
        return copies

    def send_passed(p, far_copies):
        copies = []
        for way in range(2):
            value = finish(p, nearby[way], way)
            far_copies[way].wait_recv()
            y_out[p, way, way] = (value + y_far_in[p, way].astype(F32)).astype(BF16)
            copies.append(copy(y_out.at[p, way, way], y_in.at[p, way, way], toward[way]))
        return copies

    give_part(0)
    far_a = send_far(0)
    last = send_direct(0)
    give_part(1)
    far_b = send_far(1)
    last += send_direct(1)
    last += send_passed(0, far_a)
    last += send_passed(1, far_b)
    for p in range(2):
        for half in range(2):
            rows = pl.ds(pl.multiple_of(col * 512 + half * 256, 256), 256)
            terms[rows, p * HALF:(p + 1) * HALF] = finish(p, col, half)
    wait_all(last)
    for p in range(2):
        for half in range(2):
            rows = pl.ds(pl.multiple_of(col * 512 + half * 256, 256), 256)
            total = terms[rows, p * HALF:(p + 1) * HALF] + (y_in[p, 0, half].astype(F32) + y_in[p, 1, half].astype(F32))
            out[half * 256:(half + 1) * 256, p * HALF:(p + 1) * HALF] = total.astype(BF16)
    for c in started:
        c.wait_send()


def stay(array):
    return pltpu.with_memory_space_constraint(array, pltpu.HBM)


def body(right_side, x_blocks, row_ids, col_ids, counts):
    vmem = pl.BlockSpec(memory_space=pltpu.VMEM)
    hbm = pl.BlockSpec(memory_space=pltpu.HBM)
    dense, right_t = pl.pallas_call(
        build_kernel,
        out_shape=(jax.ShapeDtypeStruct((ROWS, WIDTH), BF16), jax.ShapeDtypeStruct((COLUMNS, ROWS), BF16)),
        in_specs=[hbm, hbm, pl.BlockSpec(memory_space=pltpu.SMEM), hbm, hbm],
        out_specs=(vmem, vmem),
        scratch_shapes=[
            pltpu.VMEM((ROWS, COLUMNS), BF16),
            pltpu.VMEM((LIST_LEN, BLOCK, BLOCK), BF16),
            pltpu.VMEM((LIST_LEN // 2, BLOCK, BLOCK), F32),
            pltpu.SMEM((1, 1, LIST_LEN), jnp.int32),
            pltpu.SMEM((1, 1, LIST_LEN), jnp.int32),
            pltpu.SMEM((LIST_LEN,), jnp.int32),
            pltpu.SMEM((LIST_LEN,), jnp.int32),
            pltpu.SMEM((ROW_BLOCKS * SLOTS,), jnp.int32),
            pltpu.SMEM((LIST_LEN,), jnp.int32),
            pltpu.SMEM((LIST_LEN,), jnp.int32),
            pltpu.SMEM((LIST_LEN,), jnp.int32),
            pltpu.SemaphoreType.DMA((GROUPS + 3,)),
        ],
        compiler_params=pltpu.CompilerParams(vmem_limit_bytes=24 * 2**20),
        name="build_dense",
    )(stay(row_ids), stay(col_ids), counts, stay(right_side), stay(x_blocks))
    return pl.pallas_call(
        solve_kernel,
        out_shape=jax.ShapeDtypeStruct((ROWS // 4, COLUMNS), BF16),
        in_specs=[vmem, vmem],
        out_specs=vmem,
        scratch_shapes=[
            pltpu.VMEM((COLUMNS, 4 * BLOCK), BF16),
            pltpu.VMEM((2, 2, COLUMNS, BLOCK), BF16),
            pltpu.VMEM((2, COLUMNS, 3 * BLOCK), BF16),
            pltpu.VMEM((COLUMNS, 2 * BLOCK), F32),
            pltpu.VMEM((2, 2, COLUMNS, BLOCK), F32),
            pltpu.VMEM((COLUMNS, 3 * BLOCK), F32),
            pltpu.VMEM((COLUMNS, 3 * BLOCK), F32),
            pltpu.VMEM((COLUMNS, 3 * BLOCK), F32),
            pltpu.VMEM((2, COLUMNS, BLOCK), F32),
            pltpu.VMEM((COLUMNS, 2 * BLOCK), F32),
            pltpu.VMEM((COLUMNS, 3 * BLOCK), BF16),
            pltpu.VMEM((2, COLUMNS, BLOCK), BF16),
            pltpu.VMEM((2, Z, 16, 3 * BLOCK), BF16),
            pltpu.VMEM((2, 4, 32, BLOCK), BF16),
            pltpu.VMEM((COLUMNS, BLOCK), BF16),
            pltpu.VMEM((2, 16, 2 * BLOCK), F32),
            pltpu.VMEM((2, X, 16, 2 * BLOCK), F32),
            pltpu.VMEM((ROWS, COLUMNS), F32),
            pltpu.VMEM((2, 2, 256, HALF), BF16),
            pltpu.VMEM((2, 2, 256, HALF), BF16),
            pltpu.VMEM((2, 2, 2, 256, HALF), BF16),
            pltpu.VMEM((2, 2, 2, 256, HALF), BF16),
            pltpu.SemaphoreType.DMA((COPIES,)),
            pltpu.SemaphoreType.DMA((COPIES,)),
        ],
        compiler_params=pltpu.CompilerParams(
            collective_id=0, has_side_effects=True, vmem_limit_bytes=32 * 2**20
        ),
        name="solve",
    )(dense, right_t)


def solution(mesh):
    in_specs = (
        P("leaf", None),
        P("leaf", "col", None, None, None),
        P("leaf", "col", None),
        P("leaf", "col", None),
        P("leaf", "col"),
    )
    out_specs = P(("leaf", "col"), None)
    return jax.shard_map(body, mesh=mesh, in_specs=in_specs, out_specs=out_specs, check_vma=False)
```

```python
import jax
import jax.numpy as jnp
from jax import lax
from jax.experimental import pallas as pl
from jax.experimental.pallas import tpu as pltpu
from jax.sharding import PartitionSpec as P

BLOCK = 128
ROW_BLOCKS = 16
LIST_LEN = 96
COLUMNS = 256
SLOTS = 14
ROWS = ROW_BLOCKS * BLOCK
WIDTH = SLOTS * BLOCK
Z = 8
X = 4
HALF = COLUMNS // 2
MESH = pl.DeviceIdType.MESH
GROUPS = 8
PER_GROUP = LIST_LEN // GROUPS
F32 = jnp.float32
BF16 = jnp.bfloat16


def lane_of(slot):
    level, side = slot // 2, slot % 2
    if slot >= 8:
        return (8 + side * 3 + level - 4) * BLOCK
    if slot >= 4:
        return (4 + side * 2 + level - 2) * BLOCK
    return slot * BLOCK


def build_kernel(
    row_hbm, col_hbm, count_ref, blocks_hbm, dense, block_buf, extra, row_ref, col_ref, lanes, seen, slot_of, used, sems
):
    lists = []
    for n, (source, target) in enumerate(((row_hbm, row_ref), (col_hbm, col_ref))):
        lists.append(pltpu.make_async_copy(source, target, sems.at[GROUPS + n]))
        lists[-1].start()
    fetches = []
    for g in range(GROUPS):
        part = pl.ds(g * PER_GROUP, PER_GROUP)
        fetches.append(pltpu.make_async_copy(blocks_hbm.at[0, 0, part], block_buf.at[part], sems.at[g]))
        fetches[-1].start()

    used[0] = 0
    for slot in range(SLOTS):
        lanes[slot] = lane_of(slot)

    @pl.loop(0, ROW_BLOCKS)
    def _(i):
        for c in range(SLOTS):
            seen[i * SLOTS + c] = -1

    @pl.loop(0, LIST_LEN // 16)
    def _(i):
        for n in range(16):
            slot_of[i * 16 + n] = -1

    @pl.loop(0, ROWS // 64)
    def _(i):
        dense[pl.ds(pl.multiple_of(i * 64, 64), 64), :] = jnp.zeros((64, WIDTH), BF16)

    for c in lists:
        c.wait()
    count = count_ref[0, 0]
    for g in range(GROUPS):
        fetches[g].wait()

        @pl.loop(g * PER_GROUP, jnp.clip(count, g * PER_GROUP, (g + 1) * PER_GROUP))
        def _(k):
            r = row_ref[0, 0, k]
            c = col_ref[0, 0, k]
            place = r * SLOTS + c
            first = seen[place]
            rows = pl.ds(pl.multiple_of(r * BLOCK, BLOCK), BLOCK)
            cols = pl.ds(pl.multiple_of(lanes[c], BLOCK), BLOCK)
            dense[rows, cols] = block_buf[k]
            seen[place] = jnp.where(first < 0, k, first)

            @pl.when(first >= 0)
            def _():
                slot = slot_of[first]

                @pl.when(slot < 0)
                def _():
                    n = used[0]
                    total = block_buf[first].astype(F32) + block_buf[k].astype(F32)
                    extra[n] = total
                    dense[rows, cols] = total.astype(BF16)
                    slot_of[first] = n
                    used[0] = n + 1

                @pl.when(slot >= 0)
                def _():
                    total = extra[slot] + block_buf[k].astype(F32)
                    extra[slot] = total
                    dense[rows, cols] = total.astype(BF16)


INNER = slice(0, 2 * BLOCK)
ONE = slice(2 * BLOCK, 4 * BLOCK)
MID = slice(4 * BLOCK, 8 * BLOCK)
LATE = slice(8 * BLOCK, 14 * BLOCK)
RING_ORDER = (4, 3, 5, 2, 6, 1, 7)
COPIES = 80


def dot_t(a, b):
    return lax.dot_general(a, b, (((1,), (1,)), ((), ())), preferred_element_type=F32)


def solve_kernel(
    dense, right, out,
    right_t, coarse_low, coarse_mid, coarse_late, own_one, own_mid, own_late, late_send, late_in, mid_in, one_in, late_out, mid_out,
    ring_in, quad_in, next_in, x_out, x_in,
    terms, y_far, y_far_in, y_out, y_in, send, recv,
):
    leaf = lax.axis_index("leaf")
    col = lax.axis_index("col")
    core = lax.rem(leaf, 2)
    z = lax.rem(leaf // 2, Z)
    x = leaf // (2 * Z)
    quad = z // 4
    in_quad = lax.rem(z, 4)

    def at(x_to, z_to, core_to):
        return ((x_to * Z + z_to) * 2 + core_to, col)

    partner = at(x, z, 1 - core)
    z_peer = [at(x, lax.rem(z + d, Z), core) for d in range(Z)]
    quad_peer = [at(x, quad * 4 + lax.rem(in_quad + d, 4), core) for d in range(4)]
    z_next = at(x, z + 1 - 2 * lax.rem(z, 2), core)
    x_peer = []
    for b in range(X):
        flip_0 = x + 1 - 2 * lax.rem(x, 2) if b & 1 else x
        high = flip_0 // 2
        flip_1 = flip_0 + 2 - 4 * high if b & 2 else flip_0
        x_peer.append(at(flip_1, z, core))
    up = (leaf, lax.rem(col + 1, 4))
    down = (leaf, lax.rem(col + 3, 4))

    barrier = pltpu.get_barrier_semaphore()
    peers = [z_peer[d] for d in RING_ORDER] + x_peer[1:] + [up, down, partner]
    for peer in peers:
        pl.semaphore_signal(barrier, inc=1, device_id=peer, device_id_type=MESH)

    started = []

    def copy(src, dst, to):
        n = len(started)
        c = pltpu.make_async_remote_copy(
            src_ref=src, dst_ref=dst, send_sem=send.at[n], recv_sem=recv.at[n], device_id=to, device_id_type=MESH
        )
        c.start()
        started.append(c)
        return c

    def wait_all(copies):
        for c in copies:
            c.wait_recv()

    part_rows = [pl.ds(p * HALF, HALF) for p in range(2)]
    chunk = [pl.ds(pl.multiple_of(p * HALF + z * 16, 16), 16) for p in range(2)]
    quad_chunk = [pl.ds(pl.multiple_of(p * HALF + in_quad * 32, 32), 32) for p in range(2)]

    def partial(lanes):
        return lax.dot_general(right_t[...], dense[:, lanes], (((1,), (0,)), ((), ())), preferred_element_type=F32)

    @pl.loop(0, ROW_BLOCKS)
    def _(i):
        rows = pl.ds(pl.multiple_of(i * BLOCK, BLOCK), BLOCK)
        right_t[:, rows] = right[rows, :].T

    def late_lanes(side):
        return pl.ds(pl.multiple_of(LATE.start + side * 384, BLOCK), 384)

    late_send[...] = partial(late_lanes(1 - core))
    pl.semaphore_wait(barrier, len(peers))
    late_pair = [copy(late_send.at[part_rows[p]], late_in.at[part_rows[p]], partner) for p in range(2)]
    own_late[...] = partial(late_lanes(core))

    late_ring = []
    for p in range(2):
        late_pair[p].wait_recv()
        total = own_late[part_rows[p]] + late_in[part_rows[p]]
        own_late[part_rows[p]] = total
        late_out[part_rows[p]] = total.astype(BF16)
        ring = []
        for d in RING_ORDER:
            rows = pl.ds(pl.multiple_of(p * HALF + lax.rem(z + d, Z) * 16, 16), 16)
            ring.append(copy(late_out.at[rows], ring_in.at[p, d], z_peer[d]))
        late_ring.append(ring)
    value = partial(MID)
    for side in range(2):
        for n in range(2):
            own_mid[side, n] = value[:, (side * 2 + n) * BLOCK:(side * 2 + n + 1) * BLOCK]
    mid_pair = [copy(own_mid.at[1 - core, :, part_rows[p]], mid_in.at[:, part_rows[p]], partner) for p in range(2)]
    mid_quad = []
    mid_next = []
    for p in range(2):
        mid_pair[p].wait_recv()
        total = own_mid[core, :, part_rows[p]] + mid_in[:, part_rows[p]]
        own_mid[core, :, part_rows[p]] = total
        mid_out[:, part_rows[p]] = total.astype(BF16)
        quads = []
        for d in (2, 1, 3):
            rows = pl.ds(pl.multiple_of(p * HALF + lax.rem(in_quad + d, 4) * 32, 32), 32)
            quads.append(copy(mid_out.at[1, rows], quad_in.at[p, d], quad_peer[d]))
        mid_quad.append(quads)
        mid_next.append(copy(mid_out.at[0, part_rows[p]], next_in.at[part_rows[p]], z_next))
    own_one[...] = partial(ONE)
    one_pair = copy(own_one, one_in, partner)
    coarse_low[:, INNER] = partial(INNER).astype(BF16)

    x_copies = []
    for p in range(2):
        wait_all(late_ring[p])
        total = own_late[chunk[p]]
        for d in range(1, Z):
            total += ring_in[p, d].astype(F32)
        coarse_late[core, chunk[p], 0:BLOCK] = total[:, 0:BLOCK].astype(BF16)
        x_out[p] = total[:, BLOCK:3 * BLOCK]
        x_copies.append([
            copy(x_out.at[p, :, BLOCK:2 * BLOCK], x_in.at[p, 2, :, BLOCK:2 * BLOCK], x_peer[2]),
            copy(x_out.at[p], x_in.at[p, 1], x_peer[1]),
            copy(x_out.at[p, :, BLOCK:2 * BLOCK], x_in.at[p, 3, :, BLOCK:2 * BLOCK], x_peer[3]),
        ])
    late_share = []
    mid_share = []
    for p in range(2):
        wait_all(mid_quad[p])
        total = own_mid[core, 1, quad_chunk[p]]
        for d in range(1, 4):
            total += quad_in[p, d].astype(F32)
        coarse_mid[core, 1, quad_chunk[p]] = total.astype(BF16)
        at_three = coarse_mid.at[core, 1, quad_chunk[p]]
        mid_share.append([copy(at_three, at_three, quad_peer[d]) for d in (2, 1, 3)])
        wait_all(x_copies[p])
        coarse_late[core, chunk[p], BLOCK:2 * BLOCK] = (x_out[p, :, 0:BLOCK] + x_in[p, 1, :, 0:BLOCK]).astype(BF16)
        coarse_late[core, chunk[p], 2 * BLOCK:3 * BLOCK] = (
            (x_out[p, :, BLOCK:2 * BLOCK] + x_in[p, 1, :, BLOCK:2 * BLOCK])
            + (x_in[p, 2, :, BLOCK:2 * BLOCK] + x_in[p, 3, :, BLOCK:2 * BLOCK])
        ).astype(BF16)
        at_late = coarse_late.at[core, chunk[p]]
        late_share.append([copy(at_late, at_late, z_peer[d]) for d in RING_ORDER])
    one_pair.wait_recv()
    coarse_low[:, ONE] = (own_one[...] + one_in[...]).astype(BF16)

    @pl.loop(0, ROWS // 256)
    def _(i):
        rows = pl.ds(pl.multiple_of(i * 256, 256), 256)
        terms[rows, :] = dot_t(dense[rows, 0:ONE.stop], coarse_low[...])


    def give_part(p):
        mid_next[p].wait_recv()
        coarse_mid[core, 0, part_rows[p]] = (own_mid[core, 0, part_rows[p]] + next_in[part_rows[p]].astype(F32)).astype(BF16)
        wait_all(mid_share[p])
        at_mid = coarse_mid.at[core, :, part_rows[p]]
        gives = [copy(at_mid, at_mid, partner)]
        wait_all(late_share[p])
        at_late = coarse_late.at[core, part_rows[p]]
        gives.append(copy(at_late, at_late, partner))
        wait_all(gives)

    def finish(p, quarter, half):
        rows = pl.ds(pl.multiple_of(quarter * 512 + half * 256, 256), 256)
        pieces = [coarse_mid[side, n, part_rows[p]] for side in range(2) for n in range(2)]
        pieces += [coarse_late[side, part_rows[p]] for side in range(2)]
        coarse = jnp.concatenate(pieces, axis=1)
        return terms[rows, p * HALF:(p + 1) * HALF] + dot_t(dense[rows, MID.start:WIDTH], coarse)

    far = lax.rem(col + 2, 4)
    nearby = (lax.rem(col + 1, 4), lax.rem(col + 3, 4))
    toward = (up, down)

    def send_far(p):
        copies = []
        for way in range(2):
            y_far[p, way] = finish(p, far, way).astype(BF16)
            copies.append(copy(y_far.at[p, way], y_far_in.at[p, way], toward[way]))
        return copies

    def send_direct(p):
        copies = []
        for way in range(2):
            y_out[p, way, 1 - way] = finish(p, nearby[way], 1 - way).astype(BF16)
            copies.append(copy(y_out.at[p, way, 1 - way], y_in.at[p, way, 1 - way], toward[way]))
        return copies

    def send_passed(p, far_copies):
        copies = []
        for way in range(2):
            value = finish(p, nearby[way], way)
            far_copies[way].wait_recv()
            y_out[p, way, way] = (value + y_far_in[p, way].astype(F32)).astype(BF16)
            copies.append(copy(y_out.at[p, way, way], y_in.at[p, way, way], toward[way]))
        return copies

    give_part(0)
    far_a = send_far(0)
    last = send_direct(0)
    give_part(1)
    far_b = send_far(1)
    last += send_direct(1)
    last += send_passed(0, far_a)
    last += send_passed(1, far_b)
    for p in range(2):
        for half in range(2):
            rows = pl.ds(pl.multiple_of(col * 512 + half * 256, 256), 256)
            terms[rows, p * HALF:(p + 1) * HALF] = finish(p, col, half)
    wait_all(last)
    for p in range(2):
        for half in range(2):
            rows = pl.ds(pl.multiple_of(col * 512 + half * 256, 256), 256)
            total = terms[rows, p * HALF:(p + 1) * HALF] + (y_in[p, 0, half].astype(F32) + y_in[p, 1, half].astype(F32))
            out[half * 256:(half + 1) * 256, p * HALF:(p + 1) * HALF] = total.astype(BF16)
    for c in started:
        c.wait_send()


def stay(array):
    return pltpu.with_memory_space_constraint(array, pltpu.HBM)


def body(right_side, x_blocks, row_ids, col_ids, counts):
    vmem = pl.BlockSpec(memory_space=pltpu.VMEM)
    hbm = pl.BlockSpec(memory_space=pltpu.HBM)
    dense = pl.pallas_call(
        build_kernel,
        out_shape=jax.ShapeDtypeStruct((ROWS, WIDTH), BF16),
        in_specs=[hbm, hbm, pl.BlockSpec(memory_space=pltpu.SMEM), hbm],
        out_specs=vmem,
        scratch_shapes=[
            pltpu.VMEM((LIST_LEN, BLOCK, BLOCK), BF16),
            pltpu.VMEM((LIST_LEN // 2, BLOCK, BLOCK), F32),
            pltpu.SMEM((1, 1, LIST_LEN), jnp.int32),
            pltpu.SMEM((1, 1, LIST_LEN), jnp.int32),
            pltpu.SMEM((SLOTS,), jnp.int32),
            pltpu.SMEM((ROW_BLOCKS * SLOTS,), jnp.int32),
            pltpu.SMEM((LIST_LEN,), jnp.int32),
            pltpu.SMEM((1,), jnp.int32),
            pltpu.SemaphoreType.DMA((GROUPS + 2,)),
        ],
        compiler_params=pltpu.CompilerParams(vmem_limit_bytes=24 * 2**20),
        name="build_dense",
    )(stay(row_ids), stay(col_ids), counts, stay(x_blocks))
    return pl.pallas_call(
        solve_kernel,
        out_shape=jax.ShapeDtypeStruct((ROWS // 4, COLUMNS), BF16),
        in_specs=[vmem, vmem],
        out_specs=vmem,
        scratch_shapes=[
            pltpu.VMEM((COLUMNS, ROWS), BF16),
            pltpu.VMEM((COLUMNS, 4 * BLOCK), BF16),
            pltpu.VMEM((2, 2, COLUMNS, BLOCK), BF16),
            pltpu.VMEM((2, COLUMNS, 3 * BLOCK), BF16),
            pltpu.VMEM((COLUMNS, 2 * BLOCK), F32),
            pltpu.VMEM((2, 2, COLUMNS, BLOCK), F32),
            pltpu.VMEM((COLUMNS, 3 * BLOCK), F32),
            pltpu.VMEM((COLUMNS, 3 * BLOCK), F32),
            pltpu.VMEM((COLUMNS, 3 * BLOCK), F32),
            pltpu.VMEM((2, COLUMNS, BLOCK), F32),
            pltpu.VMEM((COLUMNS, 2 * BLOCK), F32),
            pltpu.VMEM((COLUMNS, 3 * BLOCK), BF16),
            pltpu.VMEM((2, COLUMNS, BLOCK), BF16),
            pltpu.VMEM((2, Z, 16, 3 * BLOCK), BF16),
            pltpu.VMEM((2, 4, 32, BLOCK), BF16),
            pltpu.VMEM((COLUMNS, BLOCK), BF16),
            pltpu.VMEM((2, 16, 2 * BLOCK), F32),
            pltpu.VMEM((2, X, 16, 2 * BLOCK), F32),
            pltpu.VMEM((ROWS, COLUMNS), F32),
            pltpu.VMEM((2, 2, 256, HALF), BF16),
            pltpu.VMEM((2, 2, 256, HALF), BF16),
            pltpu.VMEM((2, 2, 2, 256, HALF), BF16),
            pltpu.VMEM((2, 2, 2, 256, HALF), BF16),
            pltpu.SemaphoreType.DMA((COPIES,)),
            pltpu.SemaphoreType.DMA((COPIES,)),
        ],
        compiler_params=pltpu.CompilerParams(
            collective_id=0, has_side_effects=True, vmem_limit_bytes=32 * 2**20
        ),
        name="solve",
    )(dense, right_side)


def solution(mesh):
    in_specs = (
        P("leaf", None),
        P("leaf", "col", None, None, None),
        P("leaf", "col", None),
        P("leaf", "col", None),
        P("leaf", "col"),
    )
    out_specs = P(("leaf", "col"), None)
    return jax.shard_map(body, mesh=mesh, in_specs=in_specs, out_specs=out_specs, check_vma=False)
```

```python
import jax
import jax.numpy as jnp
from jax import lax
from jax.experimental import pallas as pl
from jax.experimental.pallas import tpu as pltpu
from jax.sharding import PartitionSpec as P

BLOCK = 128
ROW_BLOCKS = 16
LIST_LEN = 96
COLUMNS = 256
SLOTS = 14
ROWS = ROW_BLOCKS * BLOCK
WIDTH = SLOTS * BLOCK
Z = 8
X = 4
HALF = COLUMNS // 2
MESH = pl.DeviceIdType.MESH
GROUPS = 8
PER_GROUP = LIST_LEN // GROUPS
F32 = jnp.float32
BF16 = jnp.bfloat16


def lane_of(slot):
    level, side = slot // 2, slot % 2
    if slot >= 8:
        return (8 + side * 3 + level - 4) * BLOCK
    if slot >= 4:
        return (4 + side * 2 + level - 2) * BLOCK
    return slot * BLOCK


def build_kernel(
    row_hbm, col_hbm, count_ref, blocks_hbm, dense, block_buf, extra, row_ref, col_ref, lanes, seen, slot_of, used, sems
):
    lists = []
    for n, (source, target) in enumerate(((row_hbm, row_ref), (col_hbm, col_ref))):
        lists.append(pltpu.make_async_copy(source, target, sems.at[GROUPS + n]))
        lists[-1].start()
    fetches = []
    for g in range(GROUPS):
        part = pl.ds(g * PER_GROUP, PER_GROUP)
        fetches.append(pltpu.make_async_copy(blocks_hbm.at[0, 0, part], block_buf.at[part], sems.at[g]))
        fetches[-1].start()

    used[0] = 0
    for slot in range(SLOTS):
        lanes[slot] = lane_of(slot)

    @pl.loop(0, ROW_BLOCKS)
    def _(i):
        for c in range(SLOTS):
            seen[i * SLOTS + c] = -1

    @pl.loop(0, LIST_LEN // 16)
    def _(i):
        for n in range(16):
            slot_of[i * 16 + n] = -1

    @pl.loop(0, ROWS // 64)
    def _(i):
        dense[pl.ds(pl.multiple_of(i * 64, 64), 64), :] = jnp.zeros((64, WIDTH), BF16)

    for c in lists:
        c.wait()
    count = count_ref[0, 0]
    for g in range(GROUPS):
        fetches[g].wait()

        @pl.loop(g * PER_GROUP, jnp.clip(count, g * PER_GROUP, (g + 1) * PER_GROUP))
        def _(k):
            r = row_ref[0, 0, k]
            c = col_ref[0, 0, k]
            place = r * SLOTS + c
            first = seen[place]
            rows = pl.ds(pl.multiple_of(r * BLOCK, BLOCK), BLOCK)
            cols = pl.ds(pl.multiple_of(lanes[c], BLOCK), BLOCK)
            dense[rows, cols] = block_buf[k]
            seen[place] = jnp.where(first < 0, k, first)

            @pl.when(first >= 0)
            def _():
                slot = slot_of[first]

                @pl.when(slot < 0)
                def _():
                    n = used[0]
                    total = block_buf[first].astype(F32) + block_buf[k].astype(F32)
                    extra[n] = total
                    dense[rows, cols] = total.astype(BF16)
                    slot_of[first] = n
                    used[0] = n + 1

                @pl.when(slot >= 0)
                def _():
                    total = extra[slot] + block_buf[k].astype(F32)
                    extra[slot] = total
                    dense[rows, cols] = total.astype(BF16)


INNER = slice(0, 2 * BLOCK)
ONE = slice(2 * BLOCK, 4 * BLOCK)
MID = slice(4 * BLOCK, 8 * BLOCK)
LATE = slice(8 * BLOCK, 14 * BLOCK)
RING_ORDER = (4, 3, 5, 2, 6, 1, 7)
COPIES = 112


def dot_t(a, b):
    return lax.dot_general(a, b, (((1,), (1,)), ((), ())), preferred_element_type=F32)


def solve_kernel(
    dense, right, out,
    right_t, coarse_low, coarse_mid, coarse_four, coarse_top, own_one, own_mid, own_late, late_send, late_in, mid_in, one_in,
    four_out, top_out, mid_out, four_in, top_in, quad_in, next_in, x_out, x_in,
    terms, y_far, y_far_in, y_out, y_in, send, recv,
):
    leaf = lax.axis_index("leaf")
    col = lax.axis_index("col")
    core = lax.rem(leaf, 2)
    z = lax.rem(leaf // 2, Z)
    x = leaf // (2 * Z)
    quad = z // 4
    in_quad = lax.rem(z, 4)

    def at(x_to, z_to, core_to):
        return ((x_to * Z + z_to) * 2 + core_to, col)

    partner = at(x, z, 1 - core)
    z_peer = [at(x, lax.rem(z + d, Z), core) for d in range(Z)]
    quad_peer = [at(x, quad * 4 + lax.rem(in_quad + d, 4), core) for d in range(4)]
    z_next = at(x, z + 1 - 2 * lax.rem(z, 2), core)
    x_peer = []
    for b in range(X):
        flip_0 = x + 1 - 2 * lax.rem(x, 2) if b & 1 else x
        high = flip_0 // 2
        flip_1 = flip_0 + 2 - 4 * high if b & 2 else flip_0
        x_peer.append(at(flip_1, z, core))
    up = (leaf, lax.rem(col + 1, 4))
    down = (leaf, lax.rem(col + 3, 4))

    barrier = pltpu.get_barrier_semaphore()
    peers = [z_peer[d] for d in RING_ORDER] + x_peer[1:] + [up, down, partner]
    for peer in peers:
        pl.semaphore_signal(barrier, inc=1, device_id=peer, device_id_type=MESH)

    started = []

    def copy(src, dst, to):
        n = len(started)
        c = pltpu.make_async_remote_copy(
            src_ref=src, dst_ref=dst, send_sem=send.at[n], recv_sem=recv.at[n], device_id=to, device_id_type=MESH
        )
        c.start()
        started.append(c)
        return c

    def wait_all(copies):
        for c in copies:
            c.wait_recv()

    part_rows = [pl.ds(p * HALF, HALF) for p in range(2)]
    chunk = [pl.ds(pl.multiple_of(p * HALF + z * 16, 16), 16) for p in range(2)]
    quad_chunk = [pl.ds(pl.multiple_of(p * HALF + in_quad * 32, 32), 32) for p in range(2)]

    def partial(lanes):
        return lax.dot_general(right_t[...], dense[:, lanes], (((1,), (0,)), ((), ())), preferred_element_type=F32)

    square = (COLUMNS, COLUMNS)
    identity = (lax.broadcasted_iota(jnp.int32, square, 0) == lax.broadcasted_iota(jnp.int32, square, 1)).astype(BF16)
    for i in range(ROWS // COLUMNS):
        rows = slice(i * COLUMNS, (i + 1) * COLUMNS)
        right_t[:, rows] = dot_t(identity, right[rows, :]).astype(BF16)

    def late_lanes(side):
        return pl.ds(pl.multiple_of(LATE.start + side * 384, BLOCK), 384)

    late_send[...] = partial(late_lanes(1 - core))
    pl.semaphore_wait(barrier, len(peers))
    late_pair = [copy(late_send.at[part_rows[p]], late_in.at[part_rows[p]], partner) for p in range(2)]
    own_late[...] = partial(late_lanes(core))

    def ring_send(p, source, target):
        ring = []
        for d in RING_ORDER:
            rows = pl.ds(pl.multiple_of(p * HALF + lax.rem(z + d, Z) * 16, 16), 16)
            ring.append(copy(source.at[rows], target.at[p, d], z_peer[d]))
        return ring

    top_ring = []
    for p in range(2):
        late_pair[p].wait_recv()
        total = own_late[part_rows[p]] + late_in[part_rows[p]]
        own_late[part_rows[p]] = total
        four_out[part_rows[p]] = total[:, 0:BLOCK].astype(BF16)
        top_out[part_rows[p]] = total[:, BLOCK:3 * BLOCK].astype(BF16)
        top_ring.append(ring_send(p, top_out, top_in))
    four_ring = [ring_send(p, four_out, four_in) for p in range(2)]
    value = partial(MID)
    for side in range(2):
        for n in range(2):
            own_mid[side, n] = value[:, (side * 2 + n) * BLOCK:(side * 2 + n + 1) * BLOCK]
    mid_pair = [copy(own_mid.at[1 - core, :, part_rows[p]], mid_in.at[:, part_rows[p]], partner) for p in range(2)]
    mid_quad = []
    mid_next = []
    for p in range(2):
        mid_pair[p].wait_recv()
        total = own_mid[core, :, part_rows[p]] + mid_in[:, part_rows[p]]
        own_mid[core, :, part_rows[p]] = total
        mid_out[:, part_rows[p]] = total.astype(BF16)
        quads = []
        for d in (2, 1, 3):
            rows = pl.ds(pl.multiple_of(p * HALF + lax.rem(in_quad + d, 4) * 32, 32), 32)
            quads.append(copy(mid_out.at[1, rows], quad_in.at[p, d], quad_peer[d]))
        mid_quad.append(quads)
        mid_next.append(copy(mid_out.at[0, part_rows[p]], next_in.at[part_rows[p]], z_next))
    own_one[...] = partial(ONE)
    one_pair = copy(own_one, one_in, partner)
    coarse_low[:, INNER] = partial(INNER).astype(BF16)

    x_copies = []
    for p in range(2):
        wait_all(top_ring[p])
        total = own_late[chunk[p], BLOCK:3 * BLOCK]
        for d in range(1, Z):
            total += top_in[p, d].astype(F32)
        x_out[p] = total
        x_copies.append([
            copy(x_out.at[p, :, BLOCK:2 * BLOCK], x_in.at[p, 2, :, BLOCK:2 * BLOCK], x_peer[2]),
            copy(x_out.at[p], x_in.at[p, 1], x_peer[1]),
            copy(x_out.at[p, :, BLOCK:2 * BLOCK], x_in.at[p, 3, :, BLOCK:2 * BLOCK], x_peer[3]),
        ])
    four_share = []
    for p in range(2):
        wait_all(four_ring[p])
        total = own_late[chunk[p], 0:BLOCK]
        for d in range(1, Z):
            total += four_in[p, d].astype(F32)
        coarse_four[core, chunk[p]] = total.astype(BF16)
        at_four = coarse_four.at[core, chunk[p]]
        four_share.append([copy(at_four, at_four, z_peer[d]) for d in RING_ORDER])
    top_share = []
    mid_share = []
    for p in range(2):
        wait_all(mid_quad[p])
        total = own_mid[core, 1, quad_chunk[p]]
        for d in range(1, 4):
            total += quad_in[p, d].astype(F32)
        coarse_mid[core, 1, quad_chunk[p]] = total.astype(BF16)
        at_three = coarse_mid.at[core, 1, quad_chunk[p]]
        mid_share.append([copy(at_three, at_three, quad_peer[d]) for d in (2, 1, 3)])
        wait_all(x_copies[p])
        coarse_top[core, chunk[p], 0:BLOCK] = (x_out[p, :, 0:BLOCK] + x_in[p, 1, :, 0:BLOCK]).astype(BF16)
        coarse_top[core, chunk[p], BLOCK:2 * BLOCK] = (
            (x_out[p, :, BLOCK:2 * BLOCK] + x_in[p, 1, :, BLOCK:2 * BLOCK])
            + (x_in[p, 2, :, BLOCK:2 * BLOCK] + x_in[p, 3, :, BLOCK:2 * BLOCK])
        ).astype(BF16)
        at_top = coarse_top.at[core, chunk[p]]
        top_share.append([copy(at_top, at_top, z_peer[d]) for d in RING_ORDER])
    one_pair.wait_recv()
    coarse_low[:, ONE] = (own_one[...] + one_in[...]).astype(BF16)

    @pl.loop(0, ROWS // 256)
    def _(i):
        rows = pl.ds(pl.multiple_of(i * 256, 256), 256)
        terms[rows, :] = dot_t(dense[rows, 0:ONE.stop], coarse_low[...])


    def give_part(p):
        mid_next[p].wait_recv()
        coarse_mid[core, 0, part_rows[p]] = (own_mid[core, 0, part_rows[p]] + next_in[part_rows[p]].astype(F32)).astype(BF16)
        wait_all(mid_share[p])
        at_mid = coarse_mid.at[core, :, part_rows[p]]
        gives = [copy(at_mid, at_mid, partner)]
        wait_all(four_share[p])
        at_four = coarse_four.at[core, part_rows[p]]
        gives.append(copy(at_four, at_four, partner))
        wait_all(top_share[p])
        at_top = coarse_top.at[core, part_rows[p]]
        gives.append(copy(at_top, at_top, partner))
        wait_all(gives)

    def finish(p, quarter, half):
        rows = pl.ds(pl.multiple_of(quarter * 512 + half * 256, 256), 256)
        pieces = [coarse_mid[side, n, part_rows[p]] for side in range(2) for n in range(2)]
        for side in range(2):
            pieces += [coarse_four[side, part_rows[p]], coarse_top[side, part_rows[p]]]
        coarse = jnp.concatenate(pieces, axis=1)
        return terms[rows, p * HALF:(p + 1) * HALF] + dot_t(dense[rows, MID.start:WIDTH], coarse)

    far = lax.rem(col + 2, 4)
    nearby = (lax.rem(col + 1, 4), lax.rem(col + 3, 4))
    toward = (up, down)

    def send_far(p):
        copies = []
        for way in range(2):
            y_far[p, way] = finish(p, far, way).astype(BF16)
            copies.append(copy(y_far.at[p, way], y_far_in.at[p, way], toward[way]))
        return copies

    def send_direct(p):
        copies = []
        for way in range(2):
            y_out[p, way, 1 - way] = finish(p, nearby[way], 1 - way).astype(BF16)
            copies.append(copy(y_out.at[p, way, 1 - way], y_in.at[p, way, 1 - way], toward[way]))
        return copies

    def send_passed(p, far_copies):
        copies = []
        for way in range(2):
            value = finish(p, nearby[way], way)
            far_copies[way].wait_recv()
            y_out[p, way, way] = (value + y_far_in[p, way].astype(F32)).astype(BF16)
            copies.append(copy(y_out.at[p, way, way], y_in.at[p, way, way], toward[way]))
        return copies

    give_part(0)
    far_a = send_far(0)
    last = send_direct(0)
    give_part(1)
    far_b = send_far(1)
    last += send_direct(1)
    last += send_passed(0, far_a)
    last += send_passed(1, far_b)
    for p in range(2):
        for half in range(2):
            rows = pl.ds(pl.multiple_of(col * 512 + half * 256, 256), 256)
            terms[rows, p * HALF:(p + 1) * HALF] = finish(p, col, half)
    wait_all(last)
    for p in range(2):
        for half in range(2):
            rows = pl.ds(pl.multiple_of(col * 512 + half * 256, 256), 256)
            total = terms[rows, p * HALF:(p + 1) * HALF] + (y_in[p, 0, half].astype(F32) + y_in[p, 1, half].astype(F32))
            out[half * 256:(half + 1) * 256, p * HALF:(p + 1) * HALF] = total.astype(BF16)
    for c in started:
        c.wait_send()


def stay(array):
    return pltpu.with_memory_space_constraint(array, pltpu.HBM)


def body(right_side, x_blocks, row_ids, col_ids, counts):
    vmem = pl.BlockSpec(memory_space=pltpu.VMEM)
    hbm = pl.BlockSpec(memory_space=pltpu.HBM)
    dense = pl.pallas_call(
        build_kernel,
        out_shape=jax.ShapeDtypeStruct((ROWS, WIDTH), BF16),
        in_specs=[hbm, hbm, pl.BlockSpec(memory_space=pltpu.SMEM), hbm],
        out_specs=vmem,
        scratch_shapes=[
            pltpu.VMEM((LIST_LEN, BLOCK, BLOCK), BF16),
            pltpu.VMEM((LIST_LEN // 2, BLOCK, BLOCK), F32),
            pltpu.SMEM((1, 1, LIST_LEN), jnp.int32),
            pltpu.SMEM((1, 1, LIST_LEN), jnp.int32),
            pltpu.SMEM((SLOTS,), jnp.int32),
            pltpu.SMEM((ROW_BLOCKS * SLOTS,), jnp.int32),
            pltpu.SMEM((LIST_LEN,), jnp.int32),
            pltpu.SMEM((1,), jnp.int32),
            pltpu.SemaphoreType.DMA((GROUPS + 2,)),
        ],
        compiler_params=pltpu.CompilerParams(vmem_limit_bytes=24 * 2**20),
        name="build_dense",
    )(stay(row_ids), stay(col_ids), counts, stay(x_blocks))
    return pl.pallas_call(
        solve_kernel,
        out_shape=jax.ShapeDtypeStruct((ROWS // 4, COLUMNS), BF16),
        in_specs=[vmem, vmem],
        out_specs=vmem,
        scratch_shapes=[
            pltpu.VMEM((COLUMNS, ROWS), BF16),
            pltpu.VMEM((COLUMNS, 4 * BLOCK), BF16),
            pltpu.VMEM((2, 2, COLUMNS, BLOCK), BF16),
            pltpu.VMEM((2, COLUMNS, BLOCK), BF16),
            pltpu.VMEM((2, COLUMNS, 2 * BLOCK), BF16),
            pltpu.VMEM((COLUMNS, 2 * BLOCK), F32),
            pltpu.VMEM((2, 2, COLUMNS, BLOCK), F32),
            pltpu.VMEM((COLUMNS, 3 * BLOCK), F32),
            pltpu.VMEM((COLUMNS, 3 * BLOCK), F32),
            pltpu.VMEM((COLUMNS, 3 * BLOCK), F32),
            pltpu.VMEM((2, COLUMNS, BLOCK), F32),
            pltpu.VMEM((COLUMNS, 2 * BLOCK), F32),
            pltpu.VMEM((COLUMNS, BLOCK), BF16),
            pltpu.VMEM((COLUMNS, 2 * BLOCK), BF16),
            pltpu.VMEM((2, COLUMNS, BLOCK), BF16),
            pltpu.VMEM((2, Z, 16, BLOCK), BF16),
            pltpu.VMEM((2, Z, 16, 2 * BLOCK), BF16),
            pltpu.VMEM((2, 4, 32, BLOCK), BF16),
            pltpu.VMEM((COLUMNS, BLOCK), BF16),
            pltpu.VMEM((2, 16, 2 * BLOCK), F32),
            pltpu.VMEM((2, X, 16, 2 * BLOCK), F32),
            pltpu.VMEM((ROWS, COLUMNS), F32),
            pltpu.VMEM((2, 2, 256, HALF), BF16),
            pltpu.VMEM((2, 2, 256, HALF), BF16),
            pltpu.VMEM((2, 2, 2, 256, HALF), BF16),
            pltpu.VMEM((2, 2, 2, 256, HALF), BF16),
            pltpu.SemaphoreType.DMA((COPIES,)),
            pltpu.SemaphoreType.DMA((COPIES,)),
        ],
        compiler_params=pltpu.CompilerParams(
            collective_id=0, has_side_effects=True, vmem_limit_bytes=32 * 2**20
        ),
        name="solve",
    )(dense, right_side)


def solution(mesh):
    in_specs = (
        P("leaf", None),
        P("leaf", "col", None, None, None),
        P("leaf", "col", None),
        P("leaf", "col", None),
        P("leaf", "col"),
    )
    out_specs = P(("leaf", "col"), None)
    return jax.shard_map(body, mesh=mesh, in_specs=in_specs, out_specs=out_specs, check_vma=False)
```

```python
import jax
import jax.numpy as jnp
from jax import lax
from jax.experimental import pallas as pl
from jax.experimental.pallas import tpu as pltpu
from jax.sharding import PartitionSpec as P

BLOCK = 128
ROW_BLOCKS = 16
LIST_LEN = 96
COLUMNS = 256
SLOTS = 14
ROWS = ROW_BLOCKS * BLOCK
WIDTH = SLOTS * BLOCK
Z = 8
X = 4
HALF = COLUMNS // 2
MESH = pl.DeviceIdType.MESH
GROUPS = 8
PER_GROUP = LIST_LEN // GROUPS
F32 = jnp.float32
BF16 = jnp.bfloat16


def lane_of(slot):
    level, side = slot // 2, slot % 2
    if slot >= 8:
        return (8 + side * 3 + level - 4) * BLOCK
    if slot >= 4:
        return (4 + side * 2 + level - 2) * BLOCK
    return slot * BLOCK


def build_kernel(
    row_hbm, col_hbm, count_ref, blocks_hbm, dense, block_buf, extra, row_ref, col_ref, lanes, seen, slot_of, used, sems
):
    lists = []
    for n, (source, target) in enumerate(((row_hbm, row_ref), (col_hbm, col_ref))):
        lists.append(pltpu.make_async_copy(source, target, sems.at[GROUPS + n]))
        lists[-1].start()
    fetches = []
    for g in range(GROUPS):
        part = pl.ds(g * PER_GROUP, PER_GROUP)
        fetches.append(pltpu.make_async_copy(blocks_hbm.at[0, 0, part], block_buf.at[part], sems.at[g]))
        fetches[-1].start()

    used[0] = 0
    for slot in range(SLOTS):
        lanes[slot] = lane_of(slot)

    @pl.loop(0, ROW_BLOCKS)
    def _(i):
        for c in range(SLOTS):
            seen[i * SLOTS + c] = -1

    @pl.loop(0, LIST_LEN // 16)
    def _(i):
        for n in range(16):
            slot_of[i * 16 + n] = -1

    @pl.loop(0, ROWS // 64)
    def _(i):
        dense[pl.ds(pl.multiple_of(i * 64, 64), 64), :] = jnp.zeros((64, WIDTH), BF16)

    for c in lists:
        c.wait()
    count = count_ref[0, 0]
    for g in range(GROUPS):
        fetches[g].wait()

        @pl.loop(g * PER_GROUP, jnp.clip(count, g * PER_GROUP, (g + 1) * PER_GROUP))
        def _(k):
            r = row_ref[0, 0, k]
            c = col_ref[0, 0, k]
            place = r * SLOTS + c
            first = seen[place]
            rows = pl.ds(pl.multiple_of(r * BLOCK, BLOCK), BLOCK)
            cols = pl.ds(pl.multiple_of(lanes[c], BLOCK), BLOCK)
            dense[rows, cols] = block_buf[k]
            seen[place] = jnp.where(first < 0, k, first)

            @pl.when(first >= 0)
            def _():
                slot = slot_of[first]

                @pl.when(slot < 0)
                def _():
                    n = used[0]
                    total = block_buf[first].astype(F32) + block_buf[k].astype(F32)
                    extra[n] = total
                    dense[rows, cols] = total.astype(BF16)
                    slot_of[first] = n
                    used[0] = n + 1

                @pl.when(slot >= 0)
                def _():
                    total = extra[slot] + block_buf[k].astype(F32)
                    extra[slot] = total
                    dense[rows, cols] = total.astype(BF16)


INNER = slice(0, 2 * BLOCK)
ONE = slice(2 * BLOCK, 4 * BLOCK)
MID = slice(4 * BLOCK, 8 * BLOCK)
LATE = slice(8 * BLOCK, 14 * BLOCK)
RING_ORDER = (4, 3, 5, 2, 6, 1, 7)
COPIES = 112


def dot_t(a, b):
    return lax.dot_general(a, b, (((1,), (1,)), ((), ())), preferred_element_type=F32)


def solve_kernel(
    dense, right, out,
    right_t, coarse_low, coarse_mid, coarse_four, coarse_top, own_one, own_mid, own_late, late_send, late_in, mid_in, one_in,
    four_out, top_out, mid_out, four_in, top_in, quad_in, next_in, x_out, x_in,
    terms, y_far, y_far_in, y_out, y_in, send, recv,
):
    leaf = lax.axis_index("leaf")
    col = lax.axis_index("col")
    core = lax.rem(leaf, 2)
    z = lax.rem(leaf // 2, Z)
    x = leaf // (2 * Z)
    quad = z // 4
    in_quad = lax.rem(z, 4)

    def at(x_to, z_to, core_to):
        return ((x_to * Z + z_to) * 2 + core_to, col)

    partner = at(x, z, 1 - core)
    z_peer = [at(x, lax.rem(z + d, Z), core) for d in range(Z)]
    quad_peer = [at(x, quad * 4 + lax.rem(in_quad + d, 4), core) for d in range(4)]
    z_next = at(x, z + 1 - 2 * lax.rem(z, 2), core)
    x_peer = []
    for b in range(X):
        flip_0 = x + 1 - 2 * lax.rem(x, 2) if b & 1 else x
        high = flip_0 // 2
        flip_1 = flip_0 + 2 - 4 * high if b & 2 else flip_0
        x_peer.append(at(flip_1, z, core))
    up = (leaf, lax.rem(col + 1, 4))
    down = (leaf, lax.rem(col + 3, 4))

    barrier = pltpu.get_barrier_semaphore()
    peers = [z_peer[d] for d in RING_ORDER] + x_peer[1:] + [up, down, partner]
    for peer in peers:
        pl.semaphore_signal(barrier, inc=1, device_id=peer, device_id_type=MESH)

    started = []

    def copy(src, dst, to):
        n = len(started)
        c = pltpu.make_async_remote_copy(
            src_ref=src, dst_ref=dst, send_sem=send.at[n], recv_sem=recv.at[n], device_id=to, device_id_type=MESH
        )
        c.start()
        started.append(c)
        return c

    def wait_all(copies):
        for c in copies:
            c.wait_recv()

    part_rows = [pl.ds(p * HALF, HALF) for p in range(2)]
    chunk = [pl.ds(pl.multiple_of(p * HALF + z * 16, 16), 16) for p in range(2)]
    quad_chunk = [pl.ds(pl.multiple_of(p * HALF + in_quad * 32, 32), 32) for p in range(2)]

    def partial(lanes):
        return lax.dot_general(right_t[...], dense[:, lanes], (((1,), (0,)), ((), ())), preferred_element_type=F32)

    square = (COLUMNS, COLUMNS)
    identity = (lax.broadcasted_iota(jnp.int32, square, 0) == lax.broadcasted_iota(jnp.int32, square, 1)).astype(BF16)
    for i in range(ROWS // COLUMNS):
        rows = slice(i * COLUMNS, (i + 1) * COLUMNS)
        right_t[:, rows] = dot_t(identity, right[rows, :]).astype(BF16)

    def late_lanes(side):
        return pl.ds(pl.multiple_of(LATE.start + side * 384, BLOCK), 384)

    late_send[...] = partial(late_lanes(1 - core))
    pl.semaphore_wait(barrier, len(peers))
    late_pair = [copy(late_send.at[part_rows[p]], late_in.at[part_rows[p]], partner) for p in range(2)]
    own_late[...] = partial(late_lanes(core))

    def ring_send(p, source, target):
        ring = []
        for d in RING_ORDER:
            rows = pl.ds(pl.multiple_of(p * HALF + lax.rem(z + d, Z) * 16, 16), 16)
            ring.append(copy(source.at[rows], target.at[p, d], z_peer[d]))
        return ring

    top_ring = []
    for p in range(2):
        late_pair[p].wait_recv()
        total = own_late[part_rows[p]] + late_in[part_rows[p]]
        own_late[part_rows[p]] = total
        four_out[part_rows[p]] = total[:, 0:BLOCK].astype(BF16)
        top_out[part_rows[p]] = total[:, BLOCK:3 * BLOCK].astype(BF16)
        top_ring.append(ring_send(p, top_out, top_in))
    four_ring = [ring_send(p, four_out, four_in) for p in range(2)]
    value = partial(MID)
    for side in range(2):
        for n in range(2):
            own_mid[side, n] = value[:, (side * 2 + n) * BLOCK:(side * 2 + n + 1) * BLOCK]
    mid_pair = [copy(own_mid.at[1 - core, :, part_rows[p]], mid_in.at[:, part_rows[p]], partner) for p in range(2)]
    mid_quad = []
    mid_next = []
    for p in range(2):
        mid_pair[p].wait_recv()
        total = own_mid[core, :, part_rows[p]] + mid_in[:, part_rows[p]]
        own_mid[core, :, part_rows[p]] = total
        mid_out[:, part_rows[p]] = total.astype(BF16)
        quads = []
        for d in (2, 1, 3):
            rows = pl.ds(pl.multiple_of(p * HALF + lax.rem(in_quad + d, 4) * 32, 32), 32)
            quads.append(copy(mid_out.at[1, rows], quad_in.at[p, d], quad_peer[d]))
        mid_quad.append(quads)
        mid_next.append(copy(mid_out.at[0, part_rows[p]], next_in.at[part_rows[p]], z_next))
    own_one[...] = partial(ONE)
    one_pair = copy(own_one, one_in, partner)
    coarse_low[:, INNER] = partial(INNER).astype(BF16)

    x_copies = []
    for p in range(2):
        wait_all(top_ring[p])
        total = own_late[chunk[p], BLOCK:3 * BLOCK]
        for d in range(1, Z):
            total += top_in[p, d].astype(F32)
        x_out[p] = total
        x_copies.append([
            copy(x_out.at[p, :, BLOCK:2 * BLOCK], x_in.at[p, 2, :, BLOCK:2 * BLOCK], x_peer[2]),
            copy(x_out.at[p], x_in.at[p, 1], x_peer[1]),
            copy(x_out.at[p, :, BLOCK:2 * BLOCK], x_in.at[p, 3, :, BLOCK:2 * BLOCK], x_peer[3]),
        ])
    four_share = []
    top_share = []
    mid_share = []
    for p in range(2):
        wait_all(four_ring[p])
        total = own_late[chunk[p], 0:BLOCK]
        for d in range(1, Z):
            total += four_in[p, d].astype(F32)
        coarse_four[core, chunk[p]] = total.astype(BF16)
        at_four = coarse_four.at[core, chunk[p]]
        four_share.append([copy(at_four, at_four, z_peer[d]) for d in RING_ORDER])
        wait_all(mid_quad[p])
        total = own_mid[core, 1, quad_chunk[p]]
        for d in range(1, 4):
            total += quad_in[p, d].astype(F32)
        coarse_mid[core, 1, quad_chunk[p]] = total.astype(BF16)
        at_three = coarse_mid.at[core, 1, quad_chunk[p]]
        mid_share.append([copy(at_three, at_three, quad_peer[d]) for d in (2, 1, 3)])
        wait_all(x_copies[p])
        coarse_top[core, chunk[p], 0:BLOCK] = (x_out[p, :, 0:BLOCK] + x_in[p, 1, :, 0:BLOCK]).astype(BF16)
        coarse_top[core, chunk[p], BLOCK:2 * BLOCK] = (
            (x_out[p, :, BLOCK:2 * BLOCK] + x_in[p, 1, :, BLOCK:2 * BLOCK])
            + (x_in[p, 2, :, BLOCK:2 * BLOCK] + x_in[p, 3, :, BLOCK:2 * BLOCK])
        ).astype(BF16)
        at_top = coarse_top.at[core, chunk[p]]
        top_share.append([copy(at_top, at_top, z_peer[d]) for d in RING_ORDER])
    one_pair.wait_recv()
    coarse_low[:, ONE] = (own_one[...] + one_in[...]).astype(BF16)

    @pl.loop(0, ROWS // 256)
    def _(i):
        rows = pl.ds(pl.multiple_of(i * 256, 256), 256)
        terms[rows, :] = dot_t(dense[rows, 0:ONE.stop], coarse_low[...])


    def give_part(p):
        gives = []
        wait_all(four_share[p])
        at_four = coarse_four.at[core, part_rows[p]]
        gives.append(copy(at_four, at_four, partner))
        wait_all(top_share[p])
        at_top = coarse_top.at[core, part_rows[p]]
        gives.append(copy(at_top, at_top, partner))
        mid_next[p].wait_recv()
        coarse_mid[core, 0, part_rows[p]] = (own_mid[core, 0, part_rows[p]] + next_in[part_rows[p]].astype(F32)).astype(BF16)
        wait_all(mid_share[p])
        at_mid = coarse_mid.at[core, :, part_rows[p]]
        gives.append(copy(at_mid, at_mid, partner))
        wait_all(gives)

    def finish(p, quarter, half):
        rows = pl.ds(pl.multiple_of(quarter * 512 + half * 256, 256), 256)
        pieces = [coarse_mid[side, n, part_rows[p]] for side in range(2) for n in range(2)]
        for side in range(2):
            pieces += [coarse_four[side, part_rows[p]], coarse_top[side, part_rows[p]]]
        coarse = jnp.concatenate(pieces, axis=1)
        return terms[rows, p * HALF:(p + 1) * HALF] + dot_t(dense[rows, MID.start:WIDTH], coarse)

    far = lax.rem(col + 2, 4)
    nearby = (lax.rem(col + 1, 4), lax.rem(col + 3, 4))
    toward = (up, down)

    def send_far(p):
        copies = []
        for way in range(2):
            y_far[p, way] = finish(p, far, way).astype(BF16)
            copies.append(copy(y_far.at[p, way], y_far_in.at[p, way], toward[way]))
        return copies

    def send_direct(p):
        copies = []
        for way in range(2):
            y_out[p, way, 1 - way] = finish(p, nearby[way], 1 - way).astype(BF16)
            copies.append(copy(y_out.at[p, way, 1 - way], y_in.at[p, way, 1 - way], toward[way]))
        return copies

    def send_passed(p, far_copies):
        copies = []
        for way in range(2):
            value = finish(p, nearby[way], way)
            far_copies[way].wait_recv()
            y_out[p, way, way] = (value + y_far_in[p, way].astype(F32)).astype(BF16)
            copies.append(copy(y_out.at[p, way, way], y_in.at[p, way, way], toward[way]))
        return copies

    give_part(0)
    far_a = send_far(0)
    last = send_direct(0)
    give_part(1)
    far_b = send_far(1)
    last += send_direct(1)
    last += send_passed(0, far_a)
    last += send_passed(1, far_b)
    for p in range(2):
        for half in range(2):
            rows = pl.ds(pl.multiple_of(col * 512 + half * 256, 256), 256)
            terms[rows, p * HALF:(p + 1) * HALF] = finish(p, col, half)
    wait_all(last)
    for p in range(2):
        for half in range(2):
            rows = pl.ds(pl.multiple_of(col * 512 + half * 256, 256), 256)
            total = terms[rows, p * HALF:(p + 1) * HALF] + (y_in[p, 0, half].astype(F32) + y_in[p, 1, half].astype(F32))
            out[half * 256:(half + 1) * 256, p * HALF:(p + 1) * HALF] = total.astype(BF16)
    for c in started:
        c.wait_send()


def stay(array):
    return pltpu.with_memory_space_constraint(array, pltpu.HBM)


def body(right_side, x_blocks, row_ids, col_ids, counts):
    vmem = pl.BlockSpec(memory_space=pltpu.VMEM)
    hbm = pl.BlockSpec(memory_space=pltpu.HBM)
    dense = pl.pallas_call(
        build_kernel,
        out_shape=jax.ShapeDtypeStruct((ROWS, WIDTH), BF16),
        in_specs=[hbm, hbm, pl.BlockSpec(memory_space=pltpu.SMEM), hbm],
        out_specs=vmem,
        scratch_shapes=[
            pltpu.VMEM((LIST_LEN, BLOCK, BLOCK), BF16),
            pltpu.VMEM((LIST_LEN // 2, BLOCK, BLOCK), F32),
            pltpu.SMEM((1, 1, LIST_LEN), jnp.int32),
            pltpu.SMEM((1, 1, LIST_LEN), jnp.int32),
            pltpu.SMEM((SLOTS,), jnp.int32),
            pltpu.SMEM((ROW_BLOCKS * SLOTS,), jnp.int32),
            pltpu.SMEM((LIST_LEN,), jnp.int32),
            pltpu.SMEM((1,), jnp.int32),
            pltpu.SemaphoreType.DMA((GROUPS + 2,)),
        ],
        compiler_params=pltpu.CompilerParams(vmem_limit_bytes=24 * 2**20),
        name="build_dense",
    )(stay(row_ids), stay(col_ids), counts, stay(x_blocks))
    return pl.pallas_call(
        solve_kernel,
        out_shape=jax.ShapeDtypeStruct((ROWS // 4, COLUMNS), BF16),
        in_specs=[vmem, vmem],
        out_specs=vmem,
        scratch_shapes=[
            pltpu.VMEM((COLUMNS, ROWS), BF16),
            pltpu.VMEM((COLUMNS, 4 * BLOCK), BF16),
            pltpu.VMEM((2, 2, COLUMNS, BLOCK), BF16),
            pltpu.VMEM((2, COLUMNS, BLOCK), BF16),
            pltpu.VMEM((2, COLUMNS, 2 * BLOCK), BF16),
            pltpu.VMEM((COLUMNS, 2 * BLOCK), F32),
            pltpu.VMEM((2, 2, COLUMNS, BLOCK), F32),
            pltpu.VMEM((COLUMNS, 3 * BLOCK), F32),
            pltpu.VMEM((COLUMNS, 3 * BLOCK), F32),
            pltpu.VMEM((COLUMNS, 3 * BLOCK), F32),
            pltpu.VMEM((2, COLUMNS, BLOCK), F32),
            pltpu.VMEM((COLUMNS, 2 * BLOCK), F32),
            pltpu.VMEM((COLUMNS, BLOCK), BF16),
            pltpu.VMEM((COLUMNS, 2 * BLOCK), BF16),
            pltpu.VMEM((2, COLUMNS, BLOCK), BF16),
            pltpu.VMEM((2, Z, 16, BLOCK), BF16),
            pltpu.VMEM((2, Z, 16, 2 * BLOCK), BF16),
            pltpu.VMEM((2, 4, 32, BLOCK), BF16),
            pltpu.VMEM((COLUMNS, BLOCK), BF16),
            pltpu.VMEM((2, 16, 2 * BLOCK), F32),
            pltpu.VMEM((2, X, 16, 2 * BLOCK), F32),
            pltpu.VMEM((ROWS, COLUMNS), F32),
            pltpu.VMEM((2, 2, 256, HALF), BF16),
            pltpu.VMEM((2, 2, 256, HALF), BF16),
            pltpu.VMEM((2, 2, 2, 256, HALF), BF16),
            pltpu.VMEM((2, 2, 2, 256, HALF), BF16),
            pltpu.SemaphoreType.DMA((COPIES,)),
            pltpu.SemaphoreType.DMA((COPIES,)),
        ],
        compiler_params=pltpu.CompilerParams(
            collective_id=0, has_side_effects=True, vmem_limit_bytes=32 * 2**20
        ),
        name="solve",
    )(dense, right_side)


def solution(mesh):
    in_specs = (
        P("leaf", None),
        P("leaf", "col", None, None, None),
        P("leaf", "col", None),
        P("leaf", "col", None),
        P("leaf", "col"),
    )
    out_specs = P(("leaf", "col"), None)
    return jax.shard_map(body, mesh=mesh, in_specs=in_specs, out_specs=out_specs, check_vma=False)
```

```python
import jax
import jax.numpy as jnp
from jax import lax
from jax.experimental import pallas as pl
from jax.experimental.pallas import tpu as pltpu
from jax.sharding import PartitionSpec as P

BLOCK = 128
ROW_BLOCKS = 16
LIST_LEN = 96
COLUMNS = 256
SLOTS = 14
ROWS = ROW_BLOCKS * BLOCK
WIDTH = SLOTS * BLOCK
Z = 8
X = 4
HALF = COLUMNS // 2
MESH = pl.DeviceIdType.MESH
GROUPS = 8
PER_GROUP = LIST_LEN // GROUPS
F32 = jnp.float32
BF16 = jnp.bfloat16


def lane_of(slot):
    level, side = slot // 2, slot % 2
    if slot >= 8:
        return (8 + side * 3 + level - 4) * BLOCK
    if slot >= 4:
        return (4 + side * 2 + level - 2) * BLOCK
    return slot * BLOCK


def build_kernel(
    row_hbm, col_hbm, count_ref, blocks_hbm, dense, block_buf, extra, row_ref, col_ref, lanes, seen, slot_of, used, sems
):
    lists = []
    for n, (source, target) in enumerate(((row_hbm, row_ref), (col_hbm, col_ref))):
        lists.append(pltpu.make_async_copy(source, target, sems.at[GROUPS + n]))
        lists[-1].start()
    fetches = []
    for g in range(GROUPS):
        part = pl.ds(g * PER_GROUP, PER_GROUP)
        fetches.append(pltpu.make_async_copy(blocks_hbm.at[0, 0, part], block_buf.at[part], sems.at[g]))
        fetches[-1].start()

    used[0] = 0
    for slot in range(SLOTS):
        lanes[slot] = lane_of(slot)

    @pl.loop(0, ROW_BLOCKS)
    def _(i):
        for c in range(SLOTS):
            seen[i * SLOTS + c] = -1

    @pl.loop(0, LIST_LEN // 16)
    def _(i):
        for n in range(16):
            slot_of[i * 16 + n] = -1

    @pl.loop(0, ROWS // 64)
    def _(i):
        dense[pl.ds(pl.multiple_of(i * 64, 64), 64), :] = jnp.zeros((64, WIDTH), BF16)

    for c in lists:
        c.wait()
    count = count_ref[0, 0]
    for g in range(GROUPS):
        fetches[g].wait()

        @pl.loop(g * PER_GROUP, jnp.clip(count, g * PER_GROUP, (g + 1) * PER_GROUP))
        def _(k):
            r = row_ref[0, 0, k]
            c = col_ref[0, 0, k]
            place = r * SLOTS + c
            first = seen[place]
            rows = pl.ds(pl.multiple_of(r * BLOCK, BLOCK), BLOCK)
            cols = pl.ds(pl.multiple_of(lanes[c], BLOCK), BLOCK)
            dense[rows, cols] = block_buf[k]
            seen[place] = jnp.where(first < 0, k, first)

            @pl.when(first >= 0)
            def _():
                slot = slot_of[first]

                @pl.when(slot < 0)
                def _():
                    n = used[0]
                    total = block_buf[first].astype(F32) + block_buf[k].astype(F32)
                    extra[n] = total
                    dense[rows, cols] = total.astype(BF16)
                    slot_of[first] = n
                    used[0] = n + 1

                @pl.when(slot >= 0)
                def _():
                    total = extra[slot] + block_buf[k].astype(F32)
                    extra[slot] = total
                    dense[rows, cols] = total.astype(BF16)


INNER = slice(0, 2 * BLOCK)
ONE = slice(2 * BLOCK, 4 * BLOCK)
MID = slice(4 * BLOCK, 8 * BLOCK)
LATE = slice(8 * BLOCK, 14 * BLOCK)
RING_ORDER = (4, 3, 5, 2, 6, 1, 7)
COPIES = 112


def dot_t(a, b):
    return lax.dot_general(a, b, (((1,), (1,)), ((), ())), preferred_element_type=F32)


def solve_kernel(
    dense, right, out,
    right_t, coarse_low, coarse_mid, coarse_four, coarse_top, own_one, own_mid, own_late, late_send, late_in, mid_in, one_in,
    four_out, top_out, mid_out, four_in, top_in, quad_in, next_in, x_out, x_in,
    terms, y_far, y_far_in, y_out, y_in, send, recv,
):
    leaf = lax.axis_index("leaf")
    col = lax.axis_index("col")
    core = lax.rem(leaf, 2)
    z = lax.rem(leaf // 2, Z)
    x = leaf // (2 * Z)
    quad = z // 4
    in_quad = lax.rem(z, 4)

    def at(x_to, z_to, core_to):
        return ((x_to * Z + z_to) * 2 + core_to, col)

    partner = at(x, z, 1 - core)
    z_peer = [at(x, lax.rem(z + d, Z), core) for d in range(Z)]
    quad_peer = [at(x, quad * 4 + lax.rem(in_quad + d, 4), core) for d in range(4)]
    z_next = at(x, z + 1 - 2 * lax.rem(z, 2), core)
    x_peer = []
    for b in range(X):
        flip_0 = x + 1 - 2 * lax.rem(x, 2) if b & 1 else x
        high = flip_0 // 2
        flip_1 = flip_0 + 2 - 4 * high if b & 2 else flip_0
        x_peer.append(at(flip_1, z, core))
    up = (leaf, lax.rem(col + 1, 4))
    down = (leaf, lax.rem(col + 3, 4))

    barrier = pltpu.get_barrier_semaphore()
    peers = [z_peer[d] for d in RING_ORDER] + x_peer[1:] + [up, down, partner]
    for peer in peers:
        pl.semaphore_signal(barrier, inc=1, device_id=peer, device_id_type=MESH)

    started = []

    def copy(src, dst, to):
        n = len(started)
        c = pltpu.make_async_remote_copy(
            src_ref=src, dst_ref=dst, send_sem=send.at[n], recv_sem=recv.at[n], device_id=to, device_id_type=MESH
        )
        c.start()
        started.append(c)
        return c

    def wait_all(copies):
        for c in copies:
            c.wait_recv()

    part_rows = [pl.ds(p * HALF, HALF) for p in range(2)]
    chunk = [pl.ds(pl.multiple_of(p * HALF + z * 16, 16), 16) for p in range(2)]
    quad_chunk = [pl.ds(pl.multiple_of(p * HALF + in_quad * 32, 32), 32) for p in range(2)]

    def partial(lanes):
        return lax.dot_general(right_t[...], dense[:, lanes], (((1,), (0,)), ((), ())), preferred_element_type=F32)

    square = (COLUMNS, COLUMNS)
    identity = (lax.broadcasted_iota(jnp.int32, square, 0) == lax.broadcasted_iota(jnp.int32, square, 1)).astype(BF16)
    for i in range(ROWS // COLUMNS):
        rows = slice(i * COLUMNS, (i + 1) * COLUMNS)
        right_t[:, rows] = dot_t(identity, right[rows, :]).astype(BF16)

    def late_lanes(side):
        return pl.ds(pl.multiple_of(LATE.start + side * 384, BLOCK), 384)

    late_send[...] = partial(late_lanes(1 - core))
    pl.semaphore_wait(barrier, len(peers))
    late_pair = [copy(late_send.at[part_rows[p]], late_in.at[part_rows[p]], partner) for p in range(2)]
    own_late[...] = partial(late_lanes(core))

    def ring_send(p, source, target):
        ring = []
        for d in RING_ORDER:
            rows = pl.ds(pl.multiple_of(p * HALF + lax.rem(z + d, Z) * 16, 16), 16)
            ring.append(copy(source.at[rows], target.at[p, d], z_peer[d]))
        return ring

    top_ring = []
    for p in range(2):
        late_pair[p].wait_recv()
        total = own_late[part_rows[p]] + late_in[part_rows[p]]
        own_late[part_rows[p]] = total
        four_out[part_rows[p]] = total[:, 0:BLOCK].astype(BF16)
        top_out[part_rows[p]] = total[:, BLOCK:3 * BLOCK].astype(BF16)
        top_ring.append(ring_send(p, top_out, top_in))
    four_ring = [ring_send(p, four_out, four_in) for p in range(2)]
    value = partial(MID)
    for side in range(2):
        for n in range(2):
            own_mid[side, n] = value[:, (side * 2 + n) * BLOCK:(side * 2 + n + 1) * BLOCK]
    mid_pair = [copy(own_mid.at[1 - core, :, part_rows[p]], mid_in.at[:, part_rows[p]], partner) for p in range(2)]
    mid_quad = []
    mid_next = []
    for p in range(2):
        mid_pair[p].wait_recv()
        total = own_mid[core, :, part_rows[p]] + mid_in[:, part_rows[p]]
        own_mid[core, :, part_rows[p]] = total
        mid_out[:, part_rows[p]] = total.astype(BF16)
        quads = []
        for d in (2, 1, 3):
            rows = pl.ds(pl.multiple_of(p * HALF + lax.rem(in_quad + d, 4) * 32, 32), 32)
            quads.append(copy(mid_out.at[1, rows], quad_in.at[p, d], quad_peer[d]))
        mid_quad.append(quads)
        mid_next.append(copy(mid_out.at[0, part_rows[p]], next_in.at[part_rows[p]], z_next))
    own_one[...] = partial(ONE)
    one_pair = copy(own_one, one_in, partner)
    coarse_low[:, INNER] = partial(INNER).astype(BF16)

    x_copies = []
    for p in range(2):
        wait_all(top_ring[p])
        total = own_late[chunk[p], BLOCK:3 * BLOCK]
        for d in range(1, Z):
            total += top_in[p, d].astype(F32)
        x_out[p] = total
        x_copies.append([
            copy(x_out.at[p, :, BLOCK:2 * BLOCK], x_in.at[p, 2, :, BLOCK:2 * BLOCK], x_peer[2]),
            copy(x_out.at[p], x_in.at[p, 1], x_peer[1]),
            copy(x_out.at[p, :, BLOCK:2 * BLOCK], x_in.at[p, 3, :, BLOCK:2 * BLOCK], x_peer[3]),
        ])
    four_share = []
    for p in range(2):
        wait_all(four_ring[p])
        total = own_late[chunk[p], 0:BLOCK]
        for d in range(1, Z):
            total += four_in[p, d].astype(F32)
        coarse_four[core, chunk[p]] = total.astype(BF16)
        at_four = coarse_four.at[core, chunk[p]]
        four_share.append([copy(at_four, at_four, z_peer[d]) for d in RING_ORDER])
    top_share = []
    mid_share = []
    for p in range(2):
        wait_all(mid_quad[p])
        total = own_mid[core, 1, quad_chunk[p]]
        for d in range(1, 4):
            total += quad_in[p, d].astype(F32)
        coarse_mid[core, 1, quad_chunk[p]] = total.astype(BF16)
        at_three = coarse_mid.at[core, 1, quad_chunk[p]]
        mid_share.append([copy(at_three, at_three, quad_peer[d]) for d in (2, 1, 3)])
        wait_all(x_copies[p])
        coarse_top[core, chunk[p], 0:BLOCK] = (x_out[p, :, 0:BLOCK] + x_in[p, 1, :, 0:BLOCK]).astype(BF16)
        coarse_top[core, chunk[p], BLOCK:2 * BLOCK] = (
            (x_out[p, :, BLOCK:2 * BLOCK] + x_in[p, 1, :, BLOCK:2 * BLOCK])
            + (x_in[p, 2, :, BLOCK:2 * BLOCK] + x_in[p, 3, :, BLOCK:2 * BLOCK])
        ).astype(BF16)
        at_top = coarse_top.at[core, chunk[p]]
        top_share.append([copy(at_top, at_top, z_peer[d]) for d in RING_ORDER])
    one_pair.wait_recv()
    coarse_low[:, ONE] = (own_one[...] + one_in[...]).astype(BF16)

    @pl.loop(0, ROWS // 256)
    def _(i):
        rows = pl.ds(pl.multiple_of(i * 256, 256), 256)
        terms[rows, :] = dot_t(dense[rows, 0:ONE.stop], coarse_low[...])


    def give_part(p):
        mid_next[p].wait_recv()
        coarse_mid[core, 0, part_rows[p]] = (own_mid[core, 0, part_rows[p]] + next_in[part_rows[p]].astype(F32)).astype(BF16)
        wait_all(mid_share[p])
        at_mid = coarse_mid.at[core, :, part_rows[p]]
        gives = [copy(at_mid, at_mid, partner)]
        wait_all(four_share[p])
        at_four = coarse_four.at[core, part_rows[p]]
        gives.append(copy(at_four, at_four, partner))
        wait_all(top_share[p])
        at_top = coarse_top.at[core, part_rows[p]]
        gives.append(copy(at_top, at_top, partner))
        wait_all(gives)

    def finish(p, quarter, half):
        rows = pl.ds(pl.multiple_of(quarter * 512 + half * 256, 256), 256)
        pieces = [coarse_mid[side, n, part_rows[p]] for side in range(2) for n in range(2)]
        for side in range(2):
            pieces += [coarse_four[side, part_rows[p]], coarse_top[side, part_rows[p]]]
        coarse = jnp.concatenate(pieces, axis=1)
        return terms[rows, p * HALF:(p + 1) * HALF] + dot_t(dense[rows, MID.start:WIDTH], coarse)

    far = lax.rem(col + 2, 4)
    nearby = (lax.rem(col + 1, 4), lax.rem(col + 3, 4))
    toward = (up, down)

    def send_far(p):
        copies = []
        for way in range(2):
            y_far[p, way] = finish(p, far, way).astype(BF16)
            copies.append(copy(y_far.at[p, way], y_far_in.at[p, way], toward[way]))
        return copies

    def send_direct(p):
        copies = []
        for way in range(2):
            y_out[p, way, 1 - way] = finish(p, nearby[way], 1 - way).astype(BF16)
            copies.append(copy(y_out.at[p, way, 1 - way], y_in.at[p, way, 1 - way], toward[way]))
        return copies

    def send_passed(p, far_copies):
        copies = []
        for way in range(2):
            value = finish(p, nearby[way], way)
            far_copies[way].wait_recv()
            y_out[p, way, way] = (value + y_far_in[p, way].astype(F32)).astype(BF16)
            copies.append(copy(y_out.at[p, way, way], y_in.at[p, way, way], toward[way]))
        return copies

    give_part(0)
    far_a = send_far(0)
    last = send_direct(0)
    give_part(1)
    far_b = send_far(1)
    last += send_passed(0, far_a)
    last += send_direct(1)
    last += send_passed(1, far_b)
    for p in range(2):
        for half in range(2):
            rows = pl.ds(pl.multiple_of(col * 512 + half * 256, 256), 256)
            terms[rows, p * HALF:(p + 1) * HALF] = finish(p, col, half)
    wait_all(last)
    for p in range(2):
        for half in range(2):
            rows = pl.ds(pl.multiple_of(col * 512 + half * 256, 256), 256)
            total = terms[rows, p * HALF:(p + 1) * HALF] + (y_in[p, 0, half].astype(F32) + y_in[p, 1, half].astype(F32))
            out[half * 256:(half + 1) * 256, p * HALF:(p + 1) * HALF] = total.astype(BF16)
    for c in started:
        c.wait_send()


def stay(array):
    return pltpu.with_memory_space_constraint(array, pltpu.HBM)


def body(right_side, x_blocks, row_ids, col_ids, counts):
    vmem = pl.BlockSpec(memory_space=pltpu.VMEM)
    hbm = pl.BlockSpec(memory_space=pltpu.HBM)
    dense = pl.pallas_call(
        build_kernel,
        out_shape=jax.ShapeDtypeStruct((ROWS, WIDTH), BF16),
        in_specs=[hbm, hbm, pl.BlockSpec(memory_space=pltpu.SMEM), hbm],
        out_specs=vmem,
        scratch_shapes=[
            pltpu.VMEM((LIST_LEN, BLOCK, BLOCK), BF16),
            pltpu.VMEM((LIST_LEN // 2, BLOCK, BLOCK), F32),
            pltpu.SMEM((1, 1, LIST_LEN), jnp.int32),
            pltpu.SMEM((1, 1, LIST_LEN), jnp.int32),
            pltpu.SMEM((SLOTS,), jnp.int32),
            pltpu.SMEM((ROW_BLOCKS * SLOTS,), jnp.int32),
            pltpu.SMEM((LIST_LEN,), jnp.int32),
            pltpu.SMEM((1,), jnp.int32),
            pltpu.SemaphoreType.DMA((GROUPS + 2,)),
        ],
        compiler_params=pltpu.CompilerParams(vmem_limit_bytes=24 * 2**20),
        name="build_dense",
    )(stay(row_ids), stay(col_ids), counts, stay(x_blocks))
    return pl.pallas_call(
        solve_kernel,
        out_shape=jax.ShapeDtypeStruct((ROWS // 4, COLUMNS), BF16),
        in_specs=[vmem, vmem],
        out_specs=vmem,
        scratch_shapes=[
            pltpu.VMEM((COLUMNS, ROWS), BF16),
            pltpu.VMEM((COLUMNS, 4 * BLOCK), BF16),
            pltpu.VMEM((2, 2, COLUMNS, BLOCK), BF16),
            pltpu.VMEM((2, COLUMNS, BLOCK), BF16),
            pltpu.VMEM((2, COLUMNS, 2 * BLOCK), BF16),
            pltpu.VMEM((COLUMNS, 2 * BLOCK), F32),
            pltpu.VMEM((2, 2, COLUMNS, BLOCK), F32),
            pltpu.VMEM((COLUMNS, 3 * BLOCK), F32),
            pltpu.VMEM((COLUMNS, 3 * BLOCK), F32),
            pltpu.VMEM((COLUMNS, 3 * BLOCK), F32),
            pltpu.VMEM((2, COLUMNS, BLOCK), F32),
            pltpu.VMEM((COLUMNS, 2 * BLOCK), F32),
            pltpu.VMEM((COLUMNS, BLOCK), BF16),
            pltpu.VMEM((COLUMNS, 2 * BLOCK), BF16),
            pltpu.VMEM((2, COLUMNS, BLOCK), BF16),
            pltpu.VMEM((2, Z, 16, BLOCK), BF16),
            pltpu.VMEM((2, Z, 16, 2 * BLOCK), BF16),
            pltpu.VMEM((2, 4, 32, BLOCK), BF16),
            pltpu.VMEM((COLUMNS, BLOCK), BF16),
            pltpu.VMEM((2, 16, 2 * BLOCK), F32),
            pltpu.VMEM((2, X, 16, 2 * BLOCK), F32),
            pltpu.VMEM((ROWS, COLUMNS), F32),
            pltpu.VMEM((2, 2, 256, HALF), BF16),
            pltpu.VMEM((2, 2, 256, HALF), BF16),
            pltpu.VMEM((2, 2, 2, 256, HALF), BF16),
            pltpu.VMEM((2, 2, 2, 256, HALF), BF16),
            pltpu.SemaphoreType.DMA((COPIES,)),
            pltpu.SemaphoreType.DMA((COPIES,)),
        ],
        compiler_params=pltpu.CompilerParams(
            collective_id=0, has_side_effects=True, vmem_limit_bytes=32 * 2**20
        ),
        name="solve",
    )(dense, right_side)


def solution(mesh):
    in_specs = (
        P("leaf", None),
        P("leaf", "col", None, None, None),
        P("leaf", "col", None),
        P("leaf", "col", None),
        P("leaf", "col"),
    )
    out_specs = P(("leaf", "col"), None)
    return jax.shard_map(body, mesh=mesh, in_specs=in_specs, out_specs=out_specs, check_vma=False)
```
